128 devices in a mesh: gx: 8 (over y, core), gy: 16 (over x, z).
Axes of the slice: x: 4, y: 4, z: 4, core: 2. Of those that a mesh axis runs over, the one named last changes fastest.
Arguments:
- tiles: float32 [2, 3, 65536, 128], P(None, None, ('gx', 'gy')), may hold values from -6 to 6
- tile_owner: int32 [65536, 1], P(('gx', 'gy')), may hold values from 0 to 127; in each aligned block of 512 rows (0 to 511, 512 to 1023, ...) at most 8 rows name the same one
- tile_slot: int32 [65536], P(('gx', 'gy')), may hold values from 0 to 255
- tile_count: int32 [128], P(('gx', 'gy')), may hold values from 384 to 512, as said below
- green: float32 [2, 6, 1, 2048, 2048], P(None, None, None, ('gx', 'gy')), may hold values from -6 to 6
Outputs:
- field_hat: float32 [2, 3, 1, 2048, 2048], P(None, None, None, ('gx', 'gy'))
The draws below stay inside these ranges and needn't reach their ends.
Inputs may be any that keep to these rules, and one draw needn't show every extreme that they name: `tile_owner`: within the 512 entries of one device, live or not, no owner is named by more than 8; that many is reached. `tile_count`: some device has all 512 entries live.
All inputs are finite; a program needn't handle non-finite values.
Results may differ from the reference program's by a relative error of at most 0.00007.
Values sent between devices are 32-bit elements; how exact they have to be, the bound alone decides.
A program may use at most 64 MiB of HBM per device.

```python
import math
import jax
import jax.numpy as jnp
import numpy as np

NX = 2048
NY = 2048
PLANES = 1
TILE = 128
TILES_DEV = 512
CAP = 8
TILES = 65536
SLOTS = 256
N_GX = 8
N_GY = 16
DEVICES = 128


def draw_tile_count(key, part):
    count_key = jax.random.fold_in(key, 11)
    full_key = jax.random.fold_in(key, 23)
    counts = jax.random.randint(count_key, (DEVICES,), 3 * TILES_DEV // 4, TILES_DEV + 1)
    full_device = jax.random.randint(full_key, (), 0, DEVICES)
    return jnp.where(jnp.arange(DEVICES) == full_device, TILES_DEV, counts).astype(jnp.int32)


def set_ends(result, own_key, smallest, largest):
    longest = result.shape.index(max(result.shape))
    spots = []
    for shift in (0, 1):
        where = [jax.random.randint(jax.random.fold_in(own_key, axis), (), 0, length) for axis, length in enumerate(result.shape)]
        where[longest] = (where[longest] + shift) % result.shape[longest]
        spots.append(tuple(where))
    return result.at[spots[0]].set(smallest).at[spots[1]].set(largest)


def block_scale(stream_key, dims, pieces, low, top_value):
    def one(axis_at, blocks):
        draws = jax.random.uniform(jax.random.fold_in(jax.random.fold_in(stream_key, 6), axis_at), (blocks,), jnp.float32, low / len(pieces), top_value / len(pieces))
        return jnp.repeat(jnp.exp(draws), dims[axis_at] // blocks).reshape((-1,) + (1,) * (len(dims) - axis_at - 1))

    loudness = one(*pieces[0])
    for cut in pieces[1:]:
        loudness = loudness * one(*cut)
    return loudness


def shared_out(key, own, number, rows, count, top, reach, lean):
    sequence = jax.random.permutation(key, count)
    heavy_load, ordinary = shares(count, rows * top, reach, lean, True), shares(count, rows * top, reach, lean, False)
    places = jnp.arange(count)

    def named(tallies, turn):
        used = int((tallies > 0).sum())
        fixed = max(1, used // 4)
        moved = fixed + (places - fixed + turn * (used - fixed)) % max(1, count - fixed)
        return jnp.zeros((count,), jnp.int32).at[sequence[jnp.where(places < fixed, places, moved)]].set(jnp.asarray(tallies, jnp.int32))

    tallies = jnp.where(number % 4 == 0, named(heavy_load, number // 4), named(ordinary, number - number // 4 - 1))
    mixed = jax.random.permutation(jax.random.fold_in(own, 3), count)
    giver, sink = mixed[0:count // 2 * 2:2], mixed[1:count // 2 * 2:2]
    margin = jnp.minimum(tallies[giver] - 1, reach - tallies[sink]) // 2
    margin = jnp.where((giver == sequence[0]) | (sink == sequence[0]) | (tallies[sink] == 0), 0, jnp.maximum(margin, 0))
    moved = jax.random.randint(jax.random.fold_in(own, 4), (count // 2,), 0, 1 << 20) % (margin + 1)
    tallies = tallies.at[giver].add(-moved).at[sink].add(moved)
    labels = jnp.searchsorted(jnp.cumsum(tallies), jnp.arange(rows * top), side="right").astype(jnp.int32)
    grid = labels.reshape(top, rows).T
    grid = grid[jax.random.permutation(jax.random.fold_in(own, 1), rows)]
    turn = jax.random.randint(jax.random.fold_in(own, 2), (rows, 1), 0, top)
    return jnp.take_along_axis(grid, (jnp.arange(top)[None, :] + turn) % top, axis=1)


def shares(count, total, limit, slope, full):
    loads = [(1 << 20) // math.isqrt(standing ** slope) + 1 for standing in range(1, count + 1)]
    largest = limit if full else min(limit, max(-(-total // count), total * loads[0] // sum(loads)))
    least = 1 if total - largest >= count - 1 else 0
    given, rest = [largest] + [least] * (count - 1), total - largest - least * (count - 1)
    while rest > 0:
        candidates = [i for i in range(1, count) if given[i] < largest] or [i for i in range(1, count) if given[i] < limit]
        mass, left = sum([loads[i] for i in candidates]), rest
        for i in candidates:
            more = min(limit - given[i], max(1, left * loads[i] // mass), rest)
            given[i] = given[i] + more
            rest = rest - more
    return np.array(given)


def bell_draw(own_key, extent, deviation, reach, split=(), held_as=jnp.bfloat16):
    entries = jax.random.normal(own_key, extent, jnp.float32) * deviation
    if len(split) > 0:
        entries = block_scale(own_key, extent, split, -0.22, 0.18) * entries
    return jnp.clip(entries, min=-reach, max=reach).astype(held_as)


def setup_inputs(seed: int = 0) -> dict:
    streams_of = jax.random.split(jax.random.key(seed), 6)
    tiles = bell_draw(streams_of[0], (2, 3, TILES, TILE), 1.0, 6.0, ((2, 128),), jnp.float32)
    tile_owner_keys = jax.random.split(jax.random.fold_in(streams_of[1], 1), TILES // TILES_DEV)
    tile_owner_turns = jax.random.permutation(jax.random.fold_in(streams_of[1], 3), TILES // TILES_DEV)
    tile_owner = jax.vmap(lambda own, number: shared_out(jax.random.fold_in(streams_of[1], 2), own, number, TILES_DEV, DEVICES, 1, CAP, 2))(tile_owner_keys, tile_owner_turns).reshape((TILES, 1))
    tile_slot = set_ends(jax.random.randint(streams_of[2], (TILES,), 0, SLOTS), jax.random.fold_in(streams_of[2], 1), 0, SLOTS - 1).astype(jnp.int32)
    tile_count = draw_tile_count(jax.random.fold_in(streams_of[5], 71), 0)
    green = bell_draw(streams_of[4], (2, 6, PLANES, NY, NX), 1.0, 6.0, ((3, 128),), jnp.float32)
    return dict(tiles=tiles, tile_owner=tile_owner, tile_slot=tile_slot, tile_count=tile_count, green=green)


pair_index = ((0, 3, 4), (3, 1, 5), (4, 5, 2))


def reference(tiles, tile_owner, tile_slot, tile_count, green):
    devices = N_GX * N_GY
    tile_index = jnp.arange(TILES, dtype=jnp.int32)
    is_live = (tile_index % TILES_DEV) < tile_count[tile_index // TILES_DEV]
    weight = jnp.where(is_live, 1.0, 0.0).astype(tiles.dtype)
    target = tile_owner[:, 0] * SLOTS + tile_slot
    dipole_grid = jnp.zeros((2, 3, devices * SLOTS, TILE), tiles.dtype)
    dipole_grid = dipole_grid.at[:, :, target, :].add(tiles * weight[None, None, :, None])
    x_local = NX // devices
    dipole_grid = dipole_grid.reshape(2, 3, devices, PLANES, x_local, NY)
    dipole_grid = dipole_grid.transpose(0, 1, 3, 2, 4, 5).reshape(2, 3, PLANES, NX, NY)
    complex_field = dipole_grid[0] + 1j * dipole_grid[1]
    spectrum = jnp.fft.fft2(complex_field, axes=(2, 3), norm="ortho")
    spectrum = jnp.swapaxes(spectrum, 2, 3)
    tensor = green[0] + 1j * green[1]
    mixed_rows = []
    for row_comp in range(3):
        total = tensor[pair_index[row_comp][0]] * spectrum[0]
        for col_comp in range(1, 3):
            total = total + tensor[pair_index[row_comp][col_comp]] * spectrum[col_comp]
        mixed_rows.append(total)
    mixed = jnp.stack(mixed_rows)
    return jnp.stack([jnp.real(mixed), jnp.imag(mixed)]).astype(tiles.dtype)
```

```python
import functools
import math

import jax
import jax.numpy as jnp
import numpy as np
from jax import lax
from jax.experimental import pallas as pl
from jax.experimental.pallas import tpu as pltpu
from jax.sharding import PartitionSpec as P

MESH = pl.DeviceIdType.MESH
F32, BF16, I32 = jnp.float32, jnp.bfloat16, jnp.int32
PAIRS = ((0, 3, 4), (3, 1, 5), (4, 5, 2))
HOPS = [((k * 45 % 64) // 16, (k * 45 % 64) // 4 % 4, k * 45 % 4) for k in range(1, 64)]


def halves(a):
    hi = a.astype(BF16)
    return hi, (a - hi.astype(F32)).astype(BF16)


def dot(a, b):
    return lax.dot_general(a, b, (((1,), (0,)), ((), ())), preferred_element_type=F32)


def dot_nt(a, b):
    return lax.dot_general(a, b, (((1,), (1,)), ((), ())), preferred_element_type=F32)


def times(re, im, angle):
    angle %= 16
    if angle == 0:
        return re, im
    if angle == 4:
        return im, -re
    if angle == 8:
        return -re, -im
    c, s = math.cos(2 * math.pi * angle / 16), math.sin(2 * math.pi * angle / 16)
    return re * c + im * s, im * c - re * s


def dft4(v):
    (ar, ai), (br, bi), (cr, ci), (dr, di) = v
    pr, pi, qr, qi = ar + cr, ai + ci, ar - cr, ai - ci
    rr, ri, sr, si = br + dr, bi + di, br - dr, bi - di
    return [(pr + rr, pi + ri), (qr + si, qi - sr), (pr - rr, pi - ri), (qr - si, qi + sr)]


def dft16(v):
    inner = [dft4([v[4 * a + b] for a in range(4)]) for b in range(4)]
    out = [None] * 16
    for k in range(4):
        for m, value in enumerate(dft4([times(*inner[b][k], b * k) for b in range(4)])):
            out[k + 4 * m] = value
    return out


def tables():
    n = np.arange(128)
    angle = 2 * np.pi * (n[:, None] * n[None, :] % 128) / 128
    cos, sin = np.cos(angle), np.sin(angle)
    full = np.block([[cos, sin], [-sin, cos]])
    chip = np.arange(64)
    device = [(chip // 16 * 2 + core) * 16 + chip % 16 for core in range(2)]
    y_rows = np.concatenate([np.concatenate([device[core], 128 + device[core]]) for core in range(2)])
    y_table = full[y_rows]
    x_cols = [np.concatenate([part * 128 + device[s] for part in range(2) for s in (core, 1 - core)]) for core in range(2)]
    x_table = np.stack([full[:, cols].T for cols in x_cols])
    k = np.arange(16)
    turn = 2 * np.pi * k[:, None] * n[None, :] / 2048
    y_turn = np.stack([np.cos(turn), -np.sin(turn)]) / 2048
    x_turn = np.stack([np.cos(turn), -np.sin(turn)])

    def two(a):
        hi = a.astype(np.float32).astype(jnp.bfloat16)
        return hi, (a - hi.astype(np.float64)).astype(np.float32).astype(jnp.bfloat16)

    return (*two(y_table), *two(x_table), y_turn.astype(np.float32), x_turn.astype(np.float32))


def kernel(
    owner_ref, slot_ref, count_ref, yhi_ref, ylo_ref, xhi_ref, xlo_ref, yturn_ref, xturn_ref,
    tiles_ref, green_ref, out_ref,
    tiles, green, sib, msg, arr, slots_sib, slots_in, slots_msg, slots_arr,
    one_hot, zbuf, ybuf, ysib, msg2, arr2, spec, result,
    tile_sem, green_sem, out_sem, sib_send, sib_recv, own_sem,
    e1_send, e1_recv, s_send, s_recv, y_send, y_recv, e2_send, e2_recv, own2_sem,
):
    gx, gy = lax.axis_index("gx"), lax.axis_index("gy")
    x, y, z, core = gy // 4, gx // 2, gy % 4, gx % 2
    chip = y * 16 + gy
    xs, ys, zs = ([(v + d) % 4 for d in range(4)] for v in (x, y, z))
    targets = [((ys[b] * 2 + core), (xs[a] * 4 + zs[c])) for a, b, c in HOPS]
    blocks = [ys[b] * 16 + xs[a] * 4 + zs[c] for a, b, c in HOPS]
    twin = (y * 2 + 1 - core, gy)

    def local(src, dst, sem):
        return pltpu.make_async_copy(src, dst, sem)

    def remote(src, dst, send, recv, device):
        return pltpu.make_async_remote_copy(
            src_ref=src, dst_ref=dst, send_sem=send, recv_sem=recv, device_id=device, device_id_type=MESH
        )

    load_tiles = local(tiles_ref, tiles, tile_sem)
    load_tiles.start()
    load_green = local(green_ref, green, green_sem)
    load_green.start()

    barrier = pltpu.get_barrier_semaphore()
    for device in (twin, *targets):
        pl.semaphore_signal(barrier, inc=1, device_id=device, device_id_type=MESH)

    owner = owner_ref[...]
    side = ((owner >> 4) + core) & 1
    goal = side * 64 + ((owner >> 5) << 4) + (owner & 15)
    lane = lax.broadcasted_iota(I32, (1, 512), 1)
    goal = jnp.where(lane < count_ref[...], goal, -1)
    named = jnp.where(lax.broadcasted_iota(I32, (128, 512), 0) == goal, 1.0, 0.0)
    before = jnp.where(
        lax.broadcasted_iota(I32, (512, 512), 0) < lax.broadcasted_iota(I32, (512, 512), 1), 1.0, 0.0
    )
    counts = dot(named.astype(BF16), before.astype(BF16))
    rank = jnp.sum(named * counts, axis=0, keepdims=True).astype(I32)
    row = jnp.where(goal < 0, -1, goal * 8 + rank)
    slot = slot_ref[...]
    place = ((slot & 15) << 4) + (slot >> 4) + 1
    by_rank = jnp.where((lax.broadcasted_iota(I32, (128, 512), 0) & 7) == rank, place.astype(F32), 0.0)
    slots_out = dot_nt(named.astype(BF16), by_rank.astype(BF16))
    slots_sib[...] = slots_out[64:]
    pick = jnp.where(lax.broadcasted_iota(I32, (1024, 512), 0) == row, 1.0, 0.0).astype(BF16)
    load_tiles.wait()
    for c in range(3):
        for part in range(2):
            hi, lo = halves(tiles[part, c])
            both = dot(pick, jnp.concatenate([hi, lo], axis=1))
            packed = (both[:, :128] + both[:, 128:]).reshape(128, 8, 128)
            msg[c, :, part, 0] = packed[:64]
            sib[c, :, part] = packed[64:]

    pl.semaphore_wait(barrier, 64)
    to_twin = [remote(slots_sib, slots_in, sib_send.at[3], sib_recv.at[3], twin)]
    to_twin += [remote(sib.at[c], msg.at[c, :, :, 1], sib_send.at[c], sib_recv.at[c], twin) for c in range(3)]
    for copy in to_twin:
        copy.start()
    to_twin[0].wait_recv()
    lanes = lax.broadcasted_iota(I32, (64, 128), 1)
    slots_all = jnp.where(lanes < 64, slots_out[:64], slots_in[...])
    slots_msg[:, 0, :] = slots_all
    own = [local(slots_msg.at[chip], slots_arr.at[0], own_sem.at[3])]
    own[0].start()
    for k in range(63):
        remote(slots_msg.at[blocks[k]], slots_arr.at[k + 1], s_send, s_recv, targets[k]).start()
    for c in range(3):
        to_twin[1 + c].wait_recv()
        copy = local(msg.at[c, chip], arr.at[c, 0], own_sem.at[c])
        copy.start()
        own.append(copy)
        for k in range(63):
            remote(msg.at[c, blocks[k]], arr.at[c, k + 1], e1_send.at[c], e1_recv.at[c], targets[k]).start()

    remote(slots_msg.at[pl.ds(1, 63)], slots_arr.at[pl.ds(1, 63)], s_send, s_recv, twin).wait_recv()
    own[0].wait()
    spread = jnp.where(
        lax.broadcasted_iota(I32, (1024, 64), 0) >> 4 == lax.broadcasted_iota(I32, (1024, 64), 1), 1.0, 0.0
    ).astype(BF16)
    arrived = dot(spread, slots_arr[:, 0, :].astype(BF16))
    tile_id = lax.broadcasted_iota(I32, (1024, 128), 0)
    mine = lax.broadcasted_iota(I32, (1024, 128), 1) == ((tile_id >> 3) & 1) * 64 + (tile_id & 7)
    arrived = jnp.where(mine, arrived, 0.0).astype(BF16)
    place_of = dot_nt(jnp.ones((256, 128), BF16), arrived)
    one_hot[...] = jnp.where(
        place_of == (lax.broadcasted_iota(I32, (256, 1024), 0) + 1).astype(F32), 1.0, 0.0
    ).astype(BF16)

    for c in range(3):
        remote(
            msg.at[c, pl.ds(1, 63)], arr.at[c, pl.ds(1, 63)], e1_send.at[c], e1_recv.at[c], twin
        ).wait_recv()
        own[1 + c].wait()
        slab = []
        for part in range(2):
            hi, lo = halves(arr[c, :, part].reshape(1024, 128))
            both = dot(one_hot[...], jnp.concatenate([hi, lo], axis=1))
            slab.append(both[:, :128] + both[:, 128:])
        for u in range(0, 16, 8):
            v = [(slab[0][16 * t + u : 16 * t + u + 8], slab[1][16 * t + u : 16 * t + u + 8]) for t in range(16)]
            for k, (re, im) in enumerate(dft16(v)):
                cos, sin = yturn_ref[0, k : k + 1], yturn_ref[1, k : k + 1]
                zbuf[0, pl.ds(u * 16 + k, 8, stride=16), :] = re * cos - im * sin
                zbuf[1, pl.ds(u * 16 + k, 8, stride=16), :] = re * sin + im * cos
        hi, lo = halves(jnp.concatenate([zbuf[0], zbuf[1]], axis=1))
        waves = dot_nt(yhi_ref[...], hi) + dot_nt(yhi_ref[...], lo) + dot_nt(ylo_ref[...], hi)
        ybuf[c] = waves.reshape(2, 128, 256)
        swap = remote(ybuf.at[c, 1 - core], ysib.at[c], y_send.at[c], y_recv.at[c], twin)
        swap.start()
        for half in range(2):
            if half:
                swap.wait_recv()
            for part in range(2):
                for q in range(0, 64, 8):
                    for cc in range(2):
                        spot = pl.ds(part * 64 + q, 8), pl.ds(cc * 128, 128)
                        value = ysib[(c, *spot)] if half else ybuf[(c, core, *spot)]
                        msg2[c, pl.ds(q * 8 + half * 4 + part * 2 + cc, 8, stride=8), :] = value
        local(msg2.at[c, pl.ds(chip * 8, 8)], arr2.at[c, pl.ds(chip * 8, 8)], own2_sem.at[c]).start()
        for k in range(63):
            remote(
                msg2.at[c, pl.ds(blocks[k] * 8, 8)], arr2.at[c, pl.ds(chip * 8, 8)],
                e2_send.at[c], e2_recv.at[c], targets[k],
            ).start()

    load_green.wait()
    for c in range(3):
        remote(
            msg2.at[c, pl.ds(8, 504)], arr2.at[c, pl.ds(8, 504)], e2_send.at[c], e2_recv.at[c], twin
        ).wait_recv()
        local(msg2.at[c, pl.ds(chip * 8, 8)], arr2.at[c, pl.ds(chip * 8, 8)], own2_sem.at[c]).wait()
        sources = []
        for part in range(2):
            for half in range(2):
                sources.append(
                    jnp.concatenate(
                        [arr2[c, pl.ds(half * 4 + part * 2 + cc, 64, stride=8), :] for cc in range(2)], axis=1
                    )
                )
        hi, lo = halves(jnp.concatenate(sources, axis=0).T)
        waves = dot(hi, xhi_ref[core]) + dot(lo, xhi_ref[core]) + dot(hi, xlo_ref[core])
        for k0 in range(0, 16, 8):
            v = []
            for u in range(16):
                re, im = waves[u * 16 + k0 : u * 16 + k0 + 8, :128], waves[u * 16 + k0 : u * 16 + k0 + 8, 128:]
                cos, sin = xturn_ref[0, u : u + 1], xturn_ref[1, u : u + 1]
                v.append((re * cos - im * sin, re * sin + im * cos))
            for m, (re, im) in enumerate(dft16(v)):
                spec[c, 0, k0 : k0 + 8, m * 128 : m * 128 + 128] = re
                spec[c, 1, k0 : k0 + 8, m * 128 : m * 128 + 128] = im

    def mix(m, _):
        cut = pl.ds(pl.multiple_of(m * 128, 128), 128)
        s = [(spec[c, 0, :, cut], spec[c, 1, :, cut]) for c in range(3)]
        g = [(green[0, e, 0, :, cut], green[1, e, 0, :, cut]) for e in range(6)]
        for a in range(3):
            re = sum(g[PAIRS[a][b]][0] * s[b][0] - g[PAIRS[a][b]][1] * s[b][1] for b in range(3))
            im = sum(g[PAIRS[a][b]][0] * s[b][1] + g[PAIRS[a][b]][1] * s[b][0] for b in range(3))
            result[0, a, 0, :, cut] = re
            result[1, a, 0, :, cut] = im
        return 0

    lax.fori_loop(0, 16, mix, 0)
    store = local(result, out_ref, out_sem)
    store.start()
    for copy in to_twin:
        copy.wait_send()
    remote(slots_msg.at[pl.ds(1, 63)], slots_arr.at[pl.ds(1, 63)], s_send, s_recv, twin).wait_send()
    for c in range(3):
        remote(
            msg.at[c, pl.ds(1, 63)], arr.at[c, pl.ds(1, 63)], e1_send.at[c], e1_recv.at[c], twin
        ).wait_send()
        remote(ybuf.at[c, 1 - core], ysib.at[c], y_send.at[c], y_recv.at[c], twin).wait_send()
        remote(
            msg2.at[c, pl.ds(8, 504)], arr2.at[c, pl.ds(8, 504)], e2_send.at[c], e2_recv.at[c], twin
        ).wait_send()
    store.wait()


def per_device(tiles, tile_owner, tile_slot, tile_count, green):
    dma, vmem = pltpu.SemaphoreType.DMA, pltpu.VMEM
    whole = pl.BlockSpec(memory_space=pltpu.VMEM)
    anywhere = pl.BlockSpec(memory_space=pl.ANY)
    scratch = [
        vmem((2, 3, 512, 128), F32),
        vmem((2, 6, 1, 16, 2048), F32),
        vmem((3, 64, 2, 8, 128), F32),
        vmem((3, 64, 2, 2, 8, 128), F32),
        vmem((3, 64, 2, 2, 8, 128), F32),
        vmem((64, 128), F32),
        vmem((64, 128), F32),
        vmem((64, 1, 128), F32),
        vmem((64, 1, 128), F32),
        vmem((256, 1024), BF16),
        vmem((2, 256, 128), F32),
        vmem((3, 2, 128, 256), F32),
        vmem((3, 128, 256), F32),
        vmem((3, 512, 128), F32),
        vmem((3, 512, 128), F32),
        vmem((3, 2, 16, 2048), F32),
        vmem((2, 3, 1, 16, 2048), F32),
        dma(()), dma(()), dma(()), dma((4,)), dma((4,)), dma((4,)),
        dma((3,)), dma((3,)), dma(()), dma(()), dma((3,)), dma((3,)), dma((3,)), dma((3,)), dma((3,)),
    ]
    call = pl.pallas_call(
        kernel,
        out_shape=jax.ShapeDtypeStruct((2, 3, 1, 16, 2048), F32),
        in_specs=[whole] * 9 + [anywhere] * 2,
        out_specs=anywhere,
        scratch_shapes=scratch,
        compiler_params=pltpu.CompilerParams(
            collective_id=0, has_side_effects=True, vmem_limit_bytes=48 << 20
        ),
    )
    return call(
        tile_owner.reshape(1, 512), tile_slot.reshape(1, 512), tile_count.reshape(1, 1), *tables(), tiles, green
    )


def solution(mesh):
    line = ("gx", "gy")
    in_specs = (P(None, None, line, None), P(line, None), P(line), P(line), P(None, None, None, line, None))
    return jax.shard_map(
        per_device, mesh=mesh, in_specs=in_specs, out_specs=P(None, None, None, line, None), check_vma=False
    )
```

```python
import functools
import math

import jax
import jax.numpy as jnp
import numpy as np
from jax import lax
from jax.experimental import pallas as pl
from jax.experimental.pallas import tpu as pltpu
from jax.sharding import PartitionSpec as P

MESH = pl.DeviceIdType.MESH
F32, BF16, I32 = jnp.float32, jnp.bfloat16, jnp.int32
PAIRS = ((0, 3, 4), (3, 1, 5), (4, 5, 2))
HOPS = [((k * 45 % 64) // 16, (k * 45 % 64) // 4 % 4, k * 45 % 4) for k in range(1, 64)]


def halves(a):
    hi = a.astype(BF16)
    return hi, (a - hi.astype(F32)).astype(BF16)


def dot(a, b):
    return lax.dot_general(a, b, (((1,), (0,)), ((), ())), preferred_element_type=F32)


def dot_nt(a, b):
    return lax.dot_general(a, b, (((1,), (1,)), ((), ())), preferred_element_type=F32)


def times(re, im, angle):
    angle %= 16
    if angle == 0:
        return re, im
    if angle == 4:
        return im, -re
    if angle == 8:
        return -re, -im
    c, s = math.cos(2 * math.pi * angle / 16), math.sin(2 * math.pi * angle / 16)
    return re * c + im * s, im * c - re * s


def dft4(v):
    (ar, ai), (br, bi), (cr, ci), (dr, di) = v
    pr, pi, qr, qi = ar + cr, ai + ci, ar - cr, ai - ci
    rr, ri, sr, si = br + dr, bi + di, br - dr, bi - di
    return [(pr + rr, pi + ri), (qr + si, qi - sr), (pr - rr, pi - ri), (qr - si, qi + sr)]


def dft16(v):
    inner = [dft4([v[4 * a + b] for a in range(4)]) for b in range(4)]
    out = [None] * 16
    for k in range(4):
        for m, value in enumerate(dft4([times(*inner[b][k], b * k) for b in range(4)])):
            out[k + 4 * m] = value
    return out


def tables():
    n = np.arange(128)
    angle = 2 * np.pi * (n[:, None] * n[None, :] % 128) / 128
    cos, sin = np.cos(angle), np.sin(angle)
    full = np.block([[cos, sin], [-sin, cos]])
    chip = np.arange(64)
    device = [(chip // 16 * 2 + core) * 16 + chip % 16 for core in range(2)]
    y_rows = np.concatenate([np.concatenate([device[core], 128 + device[core]]) for core in range(2)])
    y_table = full[y_rows]
    x_cols = [np.concatenate([part * 128 + device[s] for part in range(2) for s in (core, 1 - core)]) for core in range(2)]
    x_table = np.stack([full[:, cols].T for cols in x_cols])
    k = np.arange(16)
    turn = 2 * np.pi * k[:, None] * n[None, :] / 2048
    y_turn = np.stack([np.cos(turn), -np.sin(turn)]) / 2048
    x_turn = np.stack([np.cos(turn), -np.sin(turn)])

    def two(a):
        hi = a.astype(np.float32).astype(jnp.bfloat16)
        return hi, (a - hi.astype(np.float64)).astype(np.float32).astype(jnp.bfloat16)

    return (*two(y_table), *two(x_table), y_turn.astype(np.float32), x_turn.astype(np.float32))


def kernel(
    owner_hbm, slot_hbm, count_hbm, yhi_hbm, ylo_hbm, xhi_hbm, xlo_hbm, yturn_hbm, xturn_hbm,
    tiles_ref, green_ref, out_ref,
    owner_ref, slot_ref, count_ref, yhi_ref, ylo_ref, xhi_ref, xlo_ref, yturn_ref, xturn_ref,
    tiles, green, sib, msg, arr, slots_sib, slots_in, slots_msg, slots_arr,
    one_hot, zbuf, ybuf, ysib, msg2, arr2, result,
    small_sem, tile_sem, green_sem, out_sem, sib_send, sib_recv, own_sem,
    e1_send, e1_recv, s_send, s_recv, y_send, y_recv, e2_send, e2_recv, own2_sem,
):
    gx, gy = lax.axis_index("gx"), lax.axis_index("gy")
    x, y, z, core = gy // 4, gx // 2, gy % 4, gx % 2
    chip = y * 16 + gy
    xs, ys, zs = ([(v + d) % 4 for d in range(4)] for v in (x, y, z))
    targets = [((ys[b] * 2 + core), (xs[a] * 4 + zs[c])) for a, b, c in HOPS]
    blocks = [ys[b] * 16 + xs[a] * 4 + zs[c] for a, b, c in HOPS]
    twin = (y * 2 + 1 - core, gy)

    def local(src, dst, sem):
        return pltpu.make_async_copy(src, dst, sem)

    def remote(src, dst, send, recv, device):
        return pltpu.make_async_remote_copy(
            src_ref=src, dst_ref=dst, send_sem=send, recv_sem=recv, device_id=device, device_id_type=MESH
        )

    small = [
        (owner_hbm, owner_ref), (slot_hbm, slot_ref), (count_hbm, count_ref),
        (yhi_hbm, yhi_ref), (ylo_hbm, ylo_ref), (xhi_hbm.at[core], xhi_ref), (xlo_hbm.at[core], xlo_ref),
        (yturn_hbm, yturn_ref), (xturn_hbm, xturn_ref),
    ]
    small = [local(src, dst, small_sem.at[k]) for k, (src, dst) in enumerate(small)]
    load_tiles = [local(tiles_ref.at[:, c], tiles.at[:, c], tile_sem.at[c]) for c in range(3)]
    load_green = local(green_ref, green, green_sem)
    for copy in (*small[:3], *load_tiles, *small[3:], load_green):
        copy.start()

    barrier = pltpu.get_barrier_semaphore()
    for device in (twin, *targets):
        pl.semaphore_signal(barrier, inc=1, device_id=device, device_id_type=MESH)

    for copy in small[:3]:
        copy.wait()
    owner = owner_ref[...]
    side = ((owner >> 4) + core) & 1
    goal = side * 64 + ((owner >> 5) << 4) + (owner & 15)
    lane = lax.broadcasted_iota(I32, (1, 512), 1)
    goal = jnp.where(lane < count_ref[0], goal, -1)
    named = jnp.where(lax.broadcasted_iota(I32, (128, 512), 0) == goal, 1.0, 0.0)
    before = jnp.where(
        lax.broadcasted_iota(I32, (512, 512), 0) < lax.broadcasted_iota(I32, (512, 512), 1), 1.0, 0.0
    )
    counts = dot(named.astype(BF16), before.astype(BF16))
    rank = jnp.sum(named * counts, axis=0, keepdims=True).astype(I32)
    row = jnp.where(goal < 0, -1, goal * 8 + rank)
    slot = slot_ref[...]
    place = ((slot & 15) << 4) + (slot >> 4) + 1
    by_rank = jnp.where((lax.broadcasted_iota(I32, (128, 512), 0) & 7) == rank, place.astype(F32), 0.0)
    slots_out = dot_nt(named.astype(BF16), by_rank.astype(BF16))
    slots_sib[...] = slots_out[64:]
    pick = jnp.where(lax.broadcasted_iota(I32, (1024, 512), 0) == row, 1.0, 0.0).astype(BF16)

    def pack(c):
        load_tiles[c].wait()
        for part in range(2):
            hi, lo = halves(tiles[part, c])
            both = dot(pick, jnp.concatenate([hi, lo], axis=1))
            packed = (both[:, :128] + both[:, 128:]).reshape(128, 8, 128)
            msg[c, :, part, 0] = packed[:64]
            sib[c, :, part] = packed[64:]

    pack(0)

    pl.semaphore_wait(barrier, 64)
    to_twin = [remote(slots_sib, slots_in, sib_send.at[3], sib_recv.at[3], twin)]
    to_twin += [remote(sib.at[c], msg.at[c, :, :, 1], sib_send.at[c], sib_recv.at[c], twin) for c in range(3)]
    to_twin[0].start()
    to_twin[1].start()
    to_twin[0].wait_recv()
    lanes = lax.broadcasted_iota(I32, (64, 128), 1)
    slots_all = jnp.where(lanes < 64, slots_out[:64], slots_in[...])
    slots_msg[:, 0, :] = slots_all
    own = [local(slots_msg.at[chip], slots_arr.at[0], own_sem.at[3])]
    own[0].start()
    for k in range(63):
        remote(slots_msg.at[blocks[k]], slots_arr.at[k + 1], s_send, s_recv, targets[k]).start()
    for c in range(3):
        if c:
            pack(c)
            to_twin[1 + c].start()
        to_twin[1 + c].wait_recv()
        copy = local(msg.at[c, chip], arr.at[c, 0], own_sem.at[c])
        copy.start()
        own.append(copy)
        for k in range(63):
            remote(msg.at[c, blocks[k]], arr.at[c, k + 1], e1_send.at[c], e1_recv.at[c], targets[k]).start()

    for copy in small[3:]:
        copy.wait()
    remote(slots_msg.at[pl.ds(1, 63)], slots_arr.at[pl.ds(1, 63)], s_send, s_recv, twin).wait_recv()
    own[0].wait()
    spread = jnp.where(
        lax.broadcasted_iota(I32, (1024, 64), 0) >> 4 == lax.broadcasted_iota(I32, (1024, 64), 1), 1.0, 0.0
    ).astype(BF16)
    arrived = dot(spread, slots_arr[:, 0, :].astype(BF16))
    tile_id = lax.broadcasted_iota(I32, (1024, 128), 0)
    mine = lax.broadcasted_iota(I32, (1024, 128), 1) == ((tile_id >> 3) & 1) * 64 + (tile_id & 7)
    arrived = jnp.where(mine, arrived, 0.0).astype(BF16)
    place_of = dot_nt(jnp.ones((256, 128), BF16), arrived)
    one_hot[...] = jnp.where(
        place_of == (lax.broadcasted_iota(I32, (256, 1024), 0) + 1).astype(F32), 1.0, 0.0
    ).astype(BF16)

    for c in range(3):
        remote(
            msg.at[c, pl.ds(1, 63)], arr.at[c, pl.ds(1, 63)], e1_send.at[c], e1_recv.at[c], twin
        ).wait_recv()
        own[1 + c].wait()
        slab = []
        for part in range(2):
            hi, lo = halves(arr[c, :, part].reshape(1024, 128))
            both = dot(one_hot[...], jnp.concatenate([hi, lo], axis=1))
            slab.append(both[:, :128] + both[:, 128:])
        for u in range(0, 16, 8):
            v = [(slab[0][16 * t + u : 16 * t + u + 8], slab[1][16 * t + u : 16 * t + u + 8]) for t in range(16)]
            for k, (re, im) in enumerate(dft16(v)):
                cos, sin = yturn_ref[0, k : k + 1], yturn_ref[1, k : k + 1]
                zbuf[0, pl.ds(u * 16 + k, 8, stride=16), :] = re * cos - im * sin
                zbuf[1, pl.ds(u * 16 + k, 8, stride=16), :] = re * sin + im * cos
        hi, lo = halves(jnp.concatenate([zbuf[0], zbuf[1]], axis=1))
        waves = dot_nt(yhi_ref[...], hi) + dot_nt(yhi_ref[...], lo) + dot_nt(ylo_ref[...], hi)
        ybuf[c] = waves.reshape(2, 128, 256)
        swap = remote(ybuf.at[c, 1 - core], ysib.at[c], y_send.at[c], y_recv.at[c], twin)
        swap.start()
        for half in range(2):
            if half:
                swap.wait_recv()
            for part in range(2):
                for q in range(0, 64, 8):
                    for cc in range(2):
                        spot = pl.ds(part * 64 + q, 8), pl.ds(cc * 128, 128)
                        value = ysib[(c, *spot)] if half else ybuf[(c, core, *spot)]
                        msg2[c, pl.ds(q * 8 + half * 4 + part * 2 + cc, 8, stride=8), :] = value
        local(msg2.at[c, pl.ds(chip * 8, 8)], arr2.at[c, pl.ds(chip * 8, 8)], own2_sem.at[c]).start()
        for k in range(63):
            remote(
                msg2.at[c, pl.ds(blocks[k] * 8, 8)], arr2.at[c, pl.ds(chip * 8, 8)],
                e2_send.at[c], e2_recv.at[c], targets[k],
            ).start()

    load_green.wait()
    for c in range(3):
        remote(
            msg2.at[c, pl.ds(8, 504)], arr2.at[c, pl.ds(8, 504)], e2_send.at[c], e2_recv.at[c], twin
        ).wait_recv()
        local(msg2.at[c, pl.ds(chip * 8, 8)], arr2.at[c, pl.ds(chip * 8, 8)], own2_sem.at[c]).wait()
        sources = []
        for part in range(2):
            for half in range(2):
                sources.append(
                    jnp.concatenate(
                        [arr2[c, pl.ds(half * 4 + part * 2 + cc, 64, stride=8), :] for cc in range(2)], axis=1
                    )
                )
        hi, lo = halves(jnp.concatenate(sources, axis=0).T)
        waves = dot(hi, xhi_ref[...]) + dot(lo, xhi_ref[...]) + dot(hi, xlo_ref[...])
        for k0 in range(0, 16, 8):
            v = []
            for u in range(16):
                re, im = waves[u * 16 + k0 : u * 16 + k0 + 8, :128], waves[u * 16 + k0 : u * 16 + k0 + 8, 128:]
                cos, sin = xturn_ref[0, u : u + 1], xturn_ref[1, u : u + 1]
                v.append((re * cos - im * sin, re * sin + im * cos))
            for m, (re, im) in enumerate(dft16(v)):
                spot = slice(k0, k0 + 8), slice(m * 128, m * 128 + 128)
                for a in range(3):
                    g, h = (green[(part, PAIRS[a][c], 0, *spot)] for part in range(2))
                    add_re, add_im = g * re - h * im, g * im + h * re
                    if c:
                        add_re = result[(0, a, 0, *spot)] + add_re
                        add_im = result[(1, a, 0, *spot)] + add_im
                    result[(0, a, 0, *spot)] = add_re
                    result[(1, a, 0, *spot)] = add_im

    store = local(result, out_ref, out_sem)
    store.start()
    for copy in to_twin:
        copy.wait_send()
    remote(slots_msg.at[pl.ds(1, 63)], slots_arr.at[pl.ds(1, 63)], s_send, s_recv, twin).wait_send()
    for c in range(3):
        remote(
            msg.at[c, pl.ds(1, 63)], arr.at[c, pl.ds(1, 63)], e1_send.at[c], e1_recv.at[c], twin
        ).wait_send()
        remote(ybuf.at[c, 1 - core], ysib.at[c], y_send.at[c], y_recv.at[c], twin).wait_send()
        remote(
            msg2.at[c, pl.ds(8, 504)], arr2.at[c, pl.ds(8, 504)], e2_send.at[c], e2_recv.at[c], twin
        ).wait_send()
    store.wait()


def per_device(tiles, tile_owner, tile_slot, tile_count, green):
    dma, vmem = pltpu.SemaphoreType.DMA, pltpu.VMEM
    hbm = pl.BlockSpec(memory_space=pltpu.HBM)
    scratch = [
        vmem((1, 512), I32), vmem((1, 512), I32), pltpu.SMEM((1,), I32),
        vmem((256, 256), BF16), vmem((256, 256), BF16), vmem((256, 256), BF16), vmem((256, 256), BF16),
        vmem((2, 16, 128), F32), vmem((2, 16, 128), F32),
        vmem((2, 3, 512, 128), F32),
        vmem((2, 6, 1, 16, 2048), F32),
        vmem((3, 64, 2, 8, 128), F32),
        vmem((3, 64, 2, 2, 8, 128), F32),
        vmem((3, 64, 2, 2, 8, 128), F32),
        vmem((64, 128), F32),
        vmem((64, 128), F32),
        vmem((64, 1, 128), F32),
        vmem((64, 1, 128), F32),
        vmem((256, 1024), BF16),
        vmem((2, 256, 128), F32),
        vmem((3, 2, 128, 256), F32),
        vmem((3, 128, 256), F32),
        vmem((3, 512, 128), F32),
        vmem((3, 512, 128), F32),
        vmem((2, 3, 1, 16, 2048), F32),
        dma((9,)), dma((3,)), dma(()), dma(()), dma((4,)), dma((4,)), dma((4,)),
        dma((3,)), dma((3,)), dma(()), dma(()), dma((3,)), dma((3,)), dma((3,)), dma((3,)), dma((3,)),
    ]
    call = pl.pallas_call(
        kernel,
        out_shape=jax.ShapeDtypeStruct((2, 3, 1, 16, 2048), F32),
        in_specs=[hbm] * 11,
        out_specs=hbm,
        scratch_shapes=scratch,
        compiler_params=pltpu.CompilerParams(
            collective_id=0, has_side_effects=True, vmem_limit_bytes=63_400_000
        ),
    )
    return call(
        tile_owner.reshape(1, 512), tile_slot.reshape(1, 512), tile_count, *tables(), tiles, green
    )


def solution(mesh):
    line = ("gx", "gy")
    in_specs = (P(None, None, line, None), P(line, None), P(line), P(line), P(None, None, None, line, None))
    return jax.shard_map(
        per_device, mesh=mesh, in_specs=in_specs, out_specs=P(None, None, None, line, None), check_vma=False
    )
```

```python
import functools
import math

import jax
import jax.numpy as jnp
import numpy as np
from jax import lax
from jax.experimental import pallas as pl
from jax.experimental.pallas import tpu as pltpu
from jax.sharding import PartitionSpec as P

MESH = pl.DeviceIdType.MESH
F32, BF16, I32 = jnp.float32, jnp.bfloat16, jnp.int32
PAIRS = ((0, 3, 4), (3, 1, 5), (4, 5, 2))
HOPS = [((k * 45 % 64) // 16, (k * 45 % 64) // 4 % 4, k * 45 % 4) for k in range(1, 64)]
HOPS.sort(key=lambda hop: -sum(min(d, 4 - d) for d in hop))

EARLY = 2


def halves(a):
    hi = a.astype(BF16)
    return hi, (a - hi.astype(F32)).astype(BF16)


def dot(a, b):
    return lax.dot_general(a, b, (((1,), (0,)), ((), ())), preferred_element_type=F32)


def dot_nt(a, b):
    return lax.dot_general(a, b, (((1,), (1,)), ((), ())), preferred_element_type=F32)


def times(re, im, angle):
    angle %= 16
    if angle == 0:
        return re, im
    if angle == 4:
        return im, -re
    if angle == 8:
        return -re, -im
    c, s = math.cos(2 * math.pi * angle / 16), math.sin(2 * math.pi * angle / 16)
    return re * c + im * s, im * c - re * s


def dft4(v):
    (ar, ai), (br, bi), (cr, ci), (dr, di) = v
    pr, pi, qr, qi = ar + cr, ai + ci, ar - cr, ai - ci
    rr, ri, sr, si = br + dr, bi + di, br - dr, bi - di
    return [(pr + rr, pi + ri), (qr + si, qi - sr), (pr - rr, pi - ri), (qr - si, qi + sr)]


def dft16(v):
    inner = [dft4([v[4 * a + b] for a in range(4)]) for b in range(4)]
    out = [None] * 16
    for k in range(4):
        for m, value in enumerate(dft4([times(*inner[b][k], b * k) for b in range(4)])):
            out[k + 4 * m] = value
    return out


def tables():
    n = np.arange(128)
    angle = 2 * np.pi * (n[:, None] * n[None, :] % 128) / 128
    cos, sin = np.cos(angle), np.sin(angle)
    full = np.block([[cos, sin], [-sin, cos]])
    chip = np.arange(64)
    device = [(chip // 16 * 2 + core) * 16 + chip % 16 for core in range(2)]
    y_rows = np.concatenate([np.concatenate([device[core], 128 + device[core]]) for core in range(2)])
    y_table = full[y_rows]
    x_cols = [np.concatenate([part * 128 + device[s] for part in range(2) for s in (core, 1 - core)]) for core in range(2)]
    x_table = np.stack([full[:, cols].T for cols in x_cols])
    k = np.arange(16)
    turn = 2 * np.pi * k[:, None] * n[None, :] / 2048
    y_turn = np.stack([np.cos(turn), -np.sin(turn)]) / 2048
    x_turn = np.stack([np.cos(turn), -np.sin(turn)])

    def two(a):
        hi = a.astype(np.float32).astype(jnp.bfloat16)
        return hi, (a - hi.astype(np.float64)).astype(np.float32).astype(jnp.bfloat16)

    return (*two(y_table), *two(x_table), y_turn.astype(np.float32), x_turn.astype(np.float32))


def kernel(
    owner_hbm, slot_hbm, count_ref, yhi_hbm, ylo_hbm, xhi_hbm, xlo_hbm, yturn_hbm, xturn_hbm,
    tiles_ref, green_ref, result,
    owner_ref, slot_ref, yhi_ref, ylo_ref, xhi_ref, xlo_ref, yturn_ref, xturn_ref,
    tiles, green, sib, msg, arr, slots_sib, slots_in, slots_msg, slots_arr,
    one_hot, zbuf, ybuf, ysib, msg2, arr2,
    round_sem, small_sem, tile_sem, green_sem, sib_send, sib_recv, own_sem,
    e1_send, e1_recv, s_send, s_recv, y_send, y_recv, e2_send, e2_recv, own2_sem,
):
    gx, gy = lax.axis_index("gx"), lax.axis_index("gy")
    x, y, z, core = gy // 4, gx // 2, gy % 4, gx % 2
    chip = y * 16 + gy
    xs, ys, zs = ([(v + d) % 4 for d in range(4)] for v in (x, y, z))
    targets = [((ys[b] * 2 + core), (xs[a] * 4 + zs[c])) for a, b, c in HOPS]
    blocks = [ys[b] * 16 + xs[a] * 4 + zs[c] for a, b, c in HOPS]
    twin = (y * 2 + 1 - core, gy)

    def local(src, dst, sem):
        return pltpu.make_async_copy(src, dst, sem)

    def remote(src, dst, send, recv, device):
        return pltpu.make_async_remote_copy(
            src_ref=src, dst_ref=dst, send_sem=send, recv_sem=recv, device_id=device, device_id_type=MESH
        )

    small = [
        (owner_hbm, owner_ref), (slot_hbm, slot_ref),
        (yhi_hbm, yhi_ref), (ylo_hbm, ylo_ref), (xhi_hbm.at[core], xhi_ref), (xlo_hbm.at[core], xlo_ref),
        (yturn_hbm, yturn_ref), (xturn_hbm, xturn_ref),
    ]
    small = [local(src, dst, small_sem.at[k]) for k, (src, dst) in enumerate(small)]
    load_tiles = [local(tiles_ref.at[:, c], tiles.at[:, c], tile_sem.at[c]) for c in range(3)]
    load_green = local(green_ref, green, green_sem)
    for copy in (*small[:2], *load_tiles, *small[2:], load_green):
        copy.start()

    x_line = [(y * 2 + core, xs[d] * 4 + z) for d in (1, 2, 3)]
    y_line = [(ys[d] * 2 + core, gy) for d in (1, 2, 3)]
    z_line = [(gx, x * 4 + zs[d]) for d in (1, 2, 3)]

    def greet(sem, devices):
        for device in devices:
            pl.semaphore_signal(sem, inc=1, device_id=device, device_id_type=MESH)

    barrier = pltpu.get_barrier_semaphore()
    greet(barrier, (twin, *x_line, *y_line, *z_line))

    for copy in small[:2]:
        copy.wait()
    owner = owner_ref[...]
    side = ((owner >> 4) + core) & 1
    goal = side * 64 + ((owner >> 5) << 4) + (owner & 15)
    lane = lax.broadcasted_iota(I32, (1, 512), 1)
    goal = jnp.where(lane < count_ref[0], goal, -1)
    named = jnp.where(lax.broadcasted_iota(I32, (128, 512), 0) == goal, 1.0, 0.0)
    before = jnp.where(
        lax.broadcasted_iota(I32, (512, 512), 0) < lax.broadcasted_iota(I32, (512, 512), 1), 1.0, 0.0
    )
    counts = dot(named.astype(BF16), before.astype(BF16))
    rank = jnp.sum(named * counts, axis=0, keepdims=True).astype(I32)
    row = jnp.where(goal < 0, -1, goal * 8 + rank)
    slot = slot_ref[...]
    place = ((slot & 15) << 4) + (slot >> 4) + 1
    by_rank = jnp.where((lax.broadcasted_iota(I32, (128, 512), 0) & 7) == rank, place.astype(F32), 0.0)
    slots_out = dot_nt(named.astype(BF16), by_rank.astype(BF16))
    slots_sib[...] = slots_out[64:]
    pick = jnp.where(lax.broadcasted_iota(I32, (1024, 512), 0) == row, 1.0, 0.0).astype(BF16)

    def pack(c):
        load_tiles[c].wait()
        for part in range(2):
            hi, lo = halves(tiles[part, c])
            both = dot(pick, jnp.concatenate([hi, lo], axis=1))
            packed = (both[:, :128] + both[:, 128:]).reshape(128, 8, 128)
            msg[c, :, part, 0] = packed[:64]
            sib[c, :, part] = packed[64:]

    to_twin = [remote(sib.at[c], msg.at[c, :, :, 1], sib_send.at[c], sib_recv.at[c], twin) for c in range(3)]
    to_twin.append(remote(slots_sib, slots_in, sib_send.at[3], sib_recv.at[3], twin))
    own = [local(msg.at[c, chip], arr.at[c, 0], own_sem.at[c]) for c in range(3)]
    own.append(local(slots_msg.at[chip], slots_arr.at[0], own_sem.at[3]))
    pending = {(c, k) for c in range(3) for k in range(63)}

    def send(c, far):
        for k in range(63):
            if (c, k) in pending and sum(d > 0 for d in HOPS[k]) <= far:
                pending.discard((c, k))
                remote(msg.at[c, blocks[k]], arr.at[c, k + 1], e1_send.at[c], e1_recv.at[c], targets[k]).start()

    pack(0)
    pl.semaphore_wait(barrier, 10)
    greet(round_sem.at[0], (*x_line, *y_line, *z_line))
    to_twin[3].start()
    to_twin[0].start()
    pack(1)
    to_twin[1].start()
    pack(2)
    to_twin[2].start()
    pl.semaphore_wait(round_sem.at[0], 9)
    greet(round_sem.at[1], x_line)
    to_twin[0].wait_recv()
    own[0].start()
    send(0, EARLY)
    to_twin[3].wait_recv()
    lanes = lax.broadcasted_iota(I32, (64, 128), 1)
    slots_msg[:, 0, :] = jnp.where(lanes < 64, slots_out[:64], slots_in[...])
    own[3].start()
    pl.semaphore_wait(round_sem.at[1], 3)
    send(0, 3)
    for k in range(63):
        remote(slots_msg.at[blocks[k]], slots_arr.at[k + 1], s_send, s_recv, targets[k]).start()
    for c in (1, 2):
        to_twin[c].wait_recv()
        own[c].start()
        send(c, 3)

    for copy in small[2:]:
        copy.wait()
    remote(slots_msg.at[pl.ds(1, 63)], slots_arr.at[pl.ds(1, 63)], s_send, s_recv, twin).wait_recv()
    own[3].wait()
    spread = jnp.where(
        lax.broadcasted_iota(I32, (1024, 64), 0) >> 4 == lax.broadcasted_iota(I32, (1024, 64), 1), 1.0, 0.0
    ).astype(BF16)
    arrived = dot(spread, slots_arr[:, 0, :].astype(BF16))
    tile_id = lax.broadcasted_iota(I32, (1024, 128), 0)
    mine = lax.broadcasted_iota(I32, (1024, 128), 1) == ((tile_id >> 3) & 1) * 64 + (tile_id & 7)
    arrived = jnp.where(mine, arrived, 0.0).astype(BF16)
    place_of = dot_nt(jnp.ones((256, 128), BF16), arrived)
    one_hot[...] = jnp.where(
        place_of == (lax.broadcasted_iota(I32, (256, 1024), 0) + 1).astype(F32), 1.0, 0.0
    ).astype(BF16)

    for c in range(3):
        remote(
            msg.at[c, pl.ds(1, 63)], arr.at[c, pl.ds(1, 63)], e1_send.at[c], e1_recv.at[c], twin
        ).wait_recv()
        own[c].wait()
        slab = []
        for part in range(2):
            hi, lo = halves(arr[c, :, part].reshape(1024, 128))
            both = dot(one_hot[...], jnp.concatenate([hi, lo], axis=1))
            slab.append(both[:, :128] + both[:, 128:])
        for u in range(0, 16, 8):
            v = [(slab[0][16 * t + u : 16 * t + u + 8], slab[1][16 * t + u : 16 * t + u + 8]) for t in range(16)]
            for k, (re, im) in enumerate(dft16(v)):
                cos, sin = yturn_ref[0, k : k + 1], yturn_ref[1, k : k + 1]
                zbuf[0, pl.ds(u * 16 + k, 8, stride=16), :] = re * cos - im * sin
                zbuf[1, pl.ds(u * 16 + k, 8, stride=16), :] = re * sin + im * cos
        hi, lo = halves(jnp.concatenate([zbuf[0], zbuf[1]], axis=1))
        waves = dot_nt(yhi_ref[...], hi) + dot_nt(yhi_ref[...], lo) + dot_nt(ylo_ref[...], hi)
        ybuf[c] = waves.reshape(2, 128, 256)
        swap = remote(ybuf.at[c, 1 - core], ysib.at[c], y_send.at[c], y_recv.at[c], twin)
        swap.start()
        for half in range(2):
            if half:
                swap.wait_recv()
            for part in range(2):
                for q in range(0, 64, 8):
                    for cc in range(2):
                        spot = pl.ds(part * 64 + q, 8), pl.ds(cc * 128, 128)
                        value = ysib[(c, *spot)] if half else ybuf[(c, core, *spot)]
                        msg2[c, pl.ds(q * 8 + half * 4 + part * 2 + cc, 8, stride=8), :] = value
        local(msg2.at[c, pl.ds(chip * 8, 8)], arr2.at[c, pl.ds(chip * 8, 8)], own2_sem.at[c]).start()
        for k in range(63):
            remote(
                msg2.at[c, pl.ds(blocks[k] * 8, 8)], arr2.at[c, pl.ds(chip * 8, 8)],
                e2_send.at[c], e2_recv.at[c], targets[k],
            ).start()

    load_green.wait()
    for c in range(3):
        remote(
            msg2.at[c, pl.ds(8, 504)], arr2.at[c, pl.ds(8, 504)], e2_send.at[c], e2_recv.at[c], twin
        ).wait_recv()
        local(msg2.at[c, pl.ds(chip * 8, 8)], arr2.at[c, pl.ds(chip * 8, 8)], own2_sem.at[c]).wait()
        sources = []
        for part in range(2):
            for half in range(2):
                sources.append(
                    jnp.concatenate(
                        [arr2[c, pl.ds(half * 4 + part * 2 + cc, 64, stride=8), :] for cc in range(2)], axis=1
                    )
                )
        hi, lo = halves(jnp.concatenate(sources, axis=0).T)
        waves = dot(hi, xhi_ref[...]) + dot(lo, xhi_ref[...]) + dot(hi, xlo_ref[...])
        for k0 in range(0, 16, 8):
            v = []
            for u in range(16):
                re, im = waves[u * 16 + k0 : u * 16 + k0 + 8, :128], waves[u * 16 + k0 : u * 16 + k0 + 8, 128:]
                cos, sin = xturn_ref[0, u : u + 1], xturn_ref[1, u : u + 1]
                v.append((re * cos - im * sin, re * sin + im * cos))
            for m, (re, im) in enumerate(dft16(v)):
                spot = slice(k0, k0 + 8), slice(m * 128, m * 128 + 128)
                for a in range(3):
                    g, h = (green[(part, PAIRS[a][c], 0, *spot)] for part in range(2))
                    add_re, add_im = g * re - h * im, g * im + h * re
                    if c:
                        add_re = result[(0, a, 0, *spot)] + add_re
                        add_im = result[(1, a, 0, *spot)] + add_im
                    result[(0, a, 0, *spot)] = add_re
                    result[(1, a, 0, *spot)] = add_im

    for copy in to_twin:
        copy.wait_send()
    remote(slots_msg.at[pl.ds(1, 63)], slots_arr.at[pl.ds(1, 63)], s_send, s_recv, twin).wait_send()
    for c in range(3):
        remote(
            msg.at[c, pl.ds(1, 63)], arr.at[c, pl.ds(1, 63)], e1_send.at[c], e1_recv.at[c], twin
        ).wait_send()
        remote(ybuf.at[c, 1 - core], ysib.at[c], y_send.at[c], y_recv.at[c], twin).wait_send()
        remote(
            msg2.at[c, pl.ds(8, 504)], arr2.at[c, pl.ds(8, 504)], e2_send.at[c], e2_recv.at[c], twin
        ).wait_send()


def per_device(tiles, tile_owner, tile_slot, tile_count, green):
    dma, vmem = pltpu.SemaphoreType.DMA, pltpu.VMEM
    hbm = pl.BlockSpec(memory_space=pltpu.HBM)
    scratch = [
        vmem((1, 512), I32), vmem((1, 512), I32),
        vmem((256, 256), BF16), vmem((256, 256), BF16), vmem((256, 256), BF16), vmem((256, 256), BF16),
        vmem((2, 16, 128), F32), vmem((2, 16, 128), F32),
        vmem((2, 3, 512, 128), F32),
        vmem((2, 6, 1, 16, 2048), F32),
        vmem((3, 64, 2, 8, 128), F32),
        vmem((3, 64, 2, 2, 8, 128), F32),
        vmem((3, 64, 2, 2, 8, 128), F32),
        vmem((64, 128), F32),
        vmem((64, 128), F32),
        vmem((64, 1, 128), F32),
        vmem((64, 1, 128), F32),
        vmem((256, 1024), BF16),
        vmem((2, 256, 128), F32),
        vmem((3, 2, 128, 256), F32),
        vmem((3, 128, 256), F32),
        vmem((3, 512, 128), F32),
        vmem((3, 512, 128), F32),
        pltpu.SemaphoreType.REGULAR((2,)), dma((8,)), dma((3,)), dma(()), dma((4,)), dma((4,)), dma((4,)),
        dma((3,)), dma((3,)), dma(()), dma(()), dma((3,)), dma((3,)), dma((3,)), dma((3,)), dma((3,)),
    ]
    call = pl.pallas_call(
        kernel,
        out_shape=vmem((2, 3, 1, 16, 2048), F32),
        in_specs=[hbm] * 2 + [pl.BlockSpec(memory_space=pltpu.SMEM)] + [hbm] * 8,
        out_specs=pl.BlockSpec(memory_space=pltpu.VMEM),
        scratch_shapes=scratch,
        compiler_params=pltpu.CompilerParams(
            collective_id=0, has_side_effects=True, vmem_limit_bytes=48 << 20
        ),
    )
    def in_hbm(*arrays):
        return [pltpu.with_memory_space_constraint(jnp.asarray(a), pltpu.HBM) for a in arrays]

    line = in_hbm(tile_owner.reshape(1, 512), tile_slot.reshape(1, 512))
    return call(*line, tile_count, *in_hbm(*tables(), tiles, green))


def solution(mesh):
    line = ("gx", "gy")
    in_specs = (P(None, None, line, None), P(line, None), P(line), P(line), P(None, None, None, line, None))
    return jax.shard_map(
        per_device, mesh=mesh, in_specs=in_specs, out_specs=P(None, None, None, line, None), check_vma=False
    )
```

```python
import functools
import math

import jax
import jax.numpy as jnp
import numpy as np
from jax import lax
from jax.experimental import pallas as pl
from jax.experimental.pallas import tpu as pltpu
from jax.sharding import PartitionSpec as P

MESH = pl.DeviceIdType.MESH
F32, BF16, I32 = jnp.float32, jnp.bfloat16, jnp.int32
PAIRS = ((0, 3, 4), (3, 1, 5), (4, 5, 2))
HOPS = [((k * 45 % 64) // 16, (k * 45 % 64) // 4 % 4, k * 45 % 4) for k in range(1, 64)]
HOPS.sort(key=lambda hop: -sum(min(d, 4 - d) for d in hop))

EARLY = 2


def halves(a):
    hi = a.astype(BF16)
    return hi, (a - hi.astype(F32)).astype(BF16)


def dot(a, b):
    return lax.dot_general(a, b, (((1,), (0,)), ((), ())), preferred_element_type=F32)


def dot_nt(a, b):
    return lax.dot_general(a, b, (((1,), (1,)), ((), ())), preferred_element_type=F32)


def times(re, im, angle):
    angle %= 16
    if angle == 0:
        return re, im
    if angle == 4:
        return im, -re
    if angle == 8:
        return -re, -im
    c, s = math.cos(2 * math.pi * angle / 16), math.sin(2 * math.pi * angle / 16)
    return re * c + im * s, im * c - re * s


def dft4(v):
    (ar, ai), (br, bi), (cr, ci), (dr, di) = v
    pr, pi, qr, qi = ar + cr, ai + ci, ar - cr, ai - ci
    rr, ri, sr, si = br + dr, bi + di, br - dr, bi - di
    return [(pr + rr, pi + ri), (qr + si, qi - sr), (pr - rr, pi - ri), (qr - si, qi + sr)]


def dft16(v):
    inner = [dft4([v[4 * a + b] for a in range(4)]) for b in range(4)]
    out = [None] * 16
    for k in range(4):
        for m, value in enumerate(dft4([times(*inner[b][k], b * k) for b in range(4)])):
            out[k + 4 * m] = value
    return out


def tables():
    n = np.arange(128)
    angle = 2 * np.pi * (n[:, None] * n[None, :] % 128) / 128
    cos, sin = np.cos(angle), np.sin(angle)
    full = np.block([[cos, sin], [-sin, cos]])
    chip = np.arange(64)
    device = [(chip // 16 * 2 + core) * 16 + chip % 16 for core in range(2)]
    y_rows = np.concatenate([np.concatenate([device[core], 128 + device[core]]) for core in range(2)])
    y_table = full[y_rows]
    x_cols = [np.concatenate([part * 128 + device[s] for part in range(2) for s in (core, 1 - core)]) for core in range(2)]
    x_table = np.stack([full[:, cols].T for cols in x_cols])
    k = np.arange(16)
    turn = 2 * np.pi * k[:, None] * n[None, :] / 2048
    y_turn = np.stack([np.cos(turn), -np.sin(turn)]) / 2048
    x_turn = np.stack([np.cos(turn), -np.sin(turn)])

    def two(a):
        hi = a.astype(np.float32).astype(jnp.bfloat16)
        return hi, (a - hi.astype(np.float64)).astype(np.float32).astype(jnp.bfloat16)

    return (*two(y_table), *two(x_table), y_turn.astype(np.float32), x_turn.astype(np.float32))


def kernel(
    owner_hbm, slot_hbm, count_ref, yhi_hbm, ylo_hbm, xhi_hbm, xlo_hbm, yturn_hbm, xturn_hbm,
    tiles_ref, green_ref, result,
    owner_ref, slot_ref, yhi_ref, ylo_ref, xhi_ref, xlo_ref, yturn_ref, xturn_ref,
    tiles, green, sib, msg, arr, slots_sib, slots_in, slots_msg, slots_arr,
    one_hot, zbuf, ybuf, ysib, msg2, arr2,
    round_sem, small_sem, tile_sem, green_sem, sib_send, sib_recv, own_sem,
    e1_send, e1_recv, s_send, s_recv, y_send, y_recv, e2_send, e2_recv, own2_sem,
):
    gx, gy = lax.axis_index("gx"), lax.axis_index("gy")
    x, y, z, core = gy // 4, gx // 2, gy % 4, gx % 2
    chip = y * 16 + gy
    xs, ys, zs = ([(v + d) % 4 for d in range(4)] for v in (x, y, z))
    targets = [((ys[b] * 2 + core), (xs[a] * 4 + zs[c])) for a, b, c in HOPS]
    blocks = [ys[b] * 16 + xs[a] * 4 + zs[c] for a, b, c in HOPS]
    twin = (y * 2 + 1 - core, gy)

    def local(src, dst, sem):
        return pltpu.make_async_copy(src, dst, sem)

    def remote(src, dst, send, recv, device):
        return pltpu.make_async_remote_copy(
            src_ref=src, dst_ref=dst, send_sem=send, recv_sem=recv, device_id=device, device_id_type=MESH
        )

    small = [
        (owner_hbm, owner_ref), (slot_hbm, slot_ref),
        (yhi_hbm, yhi_ref), (ylo_hbm, ylo_ref), (xhi_hbm.at[core], xhi_ref), (xlo_hbm.at[core], xlo_ref),
        (yturn_hbm, yturn_ref), (xturn_hbm, xturn_ref),
    ]
    small = [local(src, dst, small_sem.at[k]) for k, (src, dst) in enumerate(small)]
    load_tiles = [local(tiles_ref.at[:, c], tiles.at[:, c], tile_sem.at[c]) for c in range(3)]
    load_green = local(green_ref, green, green_sem)
    for copy in (*small[:2], *load_tiles, *small[2:], load_green):
        copy.start()

    x_line = [(y * 2 + core, xs[d] * 4 + z) for d in (1, 2, 3)]
    y_line = [(ys[d] * 2 + core, gy) for d in (1, 2, 3)]
    z_line = [(gx, x * 4 + zs[d]) for d in (1, 2, 3)]

    def greet(sem, devices):
        for device in devices:
            pl.semaphore_signal(sem, inc=1, device_id=device, device_id_type=MESH)

    barrier = pltpu.get_barrier_semaphore()
    greet(barrier, (twin, *x_line, *y_line, *z_line))

    for copy in small[:2]:
        copy.wait()
    owner = owner_ref[...]
    side = ((owner >> 4) + core) & 1
    goal = side * 64 + ((owner >> 5) << 4) + (owner & 15)
    lane = lax.broadcasted_iota(I32, (1, 512), 1)
    goal = jnp.where(lane < count_ref[0], goal, -1)
    named = jnp.where(lax.broadcasted_iota(I32, (128, 512), 0) == goal, 1.0, 0.0)
    before = jnp.where(
        lax.broadcasted_iota(I32, (512, 512), 0) < lax.broadcasted_iota(I32, (512, 512), 1), 1.0, 0.0
    )
    counts = dot(named.astype(BF16), before.astype(BF16))
    rank = jnp.sum(named * counts, axis=0, keepdims=True).astype(I32)
    row = jnp.where(goal < 0, -1, goal * 8 + rank)
    slot = slot_ref[...]
    place = ((slot & 15) << 4) + (slot >> 4) + 1
    by_rank = jnp.where((lax.broadcasted_iota(I32, (128, 512), 0) & 7) == rank, place.astype(F32), 0.0)
    slots_out = dot_nt(named.astype(BF16), by_rank.astype(BF16))
    slots_sib[...] = slots_out[64:]
    pick = jnp.where(lax.broadcasted_iota(I32, (1024, 512), 0) == row, 1.0, 0.0).astype(BF16)

    def pack(c):
        load_tiles[c].wait()
        for part in range(2):
            hi, lo = halves(tiles[part, c])
            both = dot(pick, jnp.concatenate([hi, lo], axis=1))
            packed = (both[:, :128] + both[:, 128:]).reshape(128, 8, 128)
            msg[c, :, part, 0] = packed[:64]
            sib[c, :, part] = packed[64:]

    to_twin = [remote(sib.at[c], msg.at[c, :, :, 1], sib_send.at[c], sib_recv.at[c], twin) for c in range(3)]
    to_twin.append(remote(slots_sib, slots_in, sib_send.at[3], sib_recv.at[3], twin))
    own = [local(msg.at[c, chip], arr.at[c, 0], own_sem.at[c]) for c in range(3)]
    own.append(local(slots_msg.at[chip], slots_arr.at[0], own_sem.at[3]))
    pending = {(c, k) for c in range(3) for k in range(63)}

    def send(c, far):
        for k in range(63):
            if (c, k) in pending and sum(d > 0 for d in HOPS[k]) <= far:
                pending.discard((c, k))
                remote(msg.at[c, blocks[k]], arr.at[c, k + 1], e1_send.at[c], e1_recv.at[c], targets[k]).start()
                if c == 1:
                    remote(slots_msg.at[blocks[k]], slots_arr.at[k + 1], s_send, s_recv, targets[k]).start()

    pack(0)
    pl.semaphore_wait(barrier, 10)
    greet(round_sem.at[0], (*x_line, *y_line, *z_line))
    to_twin[3].start()
    to_twin[0].start()
    pack(1)
    to_twin[1].start()
    pack(2)
    to_twin[2].start()
    pl.semaphore_wait(round_sem.at[0], 9)
    greet(round_sem.at[1], x_line)
    to_twin[0].wait_recv()
    own[0].start()
    send(0, EARLY)
    to_twin[3].wait_recv()
    lanes = lax.broadcasted_iota(I32, (64, 128), 1)
    slots_msg[:, 0, :] = jnp.where(lanes < 64, slots_out[:64], slots_in[...])
    own[3].start()
    pl.semaphore_wait(round_sem.at[1], 3)
    send(0, 3)
    for c in (1, 2):
        to_twin[c].wait_recv()
        own[c].start()
        send(c, 3)

    for copy in small[2:]:
        copy.wait()
    remote(slots_msg.at[pl.ds(1, 63)], slots_arr.at[pl.ds(1, 63)], s_send, s_recv, twin).wait_recv()
    own[3].wait()
    spread = jnp.where(
        lax.broadcasted_iota(I32, (1024, 64), 0) >> 4 == lax.broadcasted_iota(I32, (1024, 64), 1), 1.0, 0.0
    ).astype(BF16)
    arrived = dot(spread, slots_arr[:, 0, :].astype(BF16))
    tile_id = lax.broadcasted_iota(I32, (1024, 128), 0)
    mine = lax.broadcasted_iota(I32, (1024, 128), 1) == ((tile_id >> 3) & 1) * 64 + (tile_id & 7)
    arrived = jnp.where(mine, arrived, 0.0).astype(BF16)
    place_of = dot_nt(jnp.ones((256, 128), BF16), arrived)
    one_hot[...] = jnp.where(
        place_of == (lax.broadcasted_iota(I32, (256, 1024), 0) + 1).astype(F32), 1.0, 0.0
    ).astype(BF16)

    for c in range(3):
        remote(
            msg.at[c, pl.ds(1, 63)], arr.at[c, pl.ds(1, 63)], e1_send.at[c], e1_recv.at[c], twin
        ).wait_recv()
        own[c].wait()
        slab = []
        for part in range(2):
            hi, lo = halves(arr[c, :, part].reshape(1024, 128))
            both = dot(one_hot[...], jnp.concatenate([hi, lo], axis=1))
            slab.append(both[:, :128] + both[:, 128:])
        for u in range(0, 16, 8):
            v = [(slab[0][16 * t + u : 16 * t + u + 8], slab[1][16 * t + u : 16 * t + u + 8]) for t in range(16)]
            for k, (re, im) in enumerate(dft16(v)):
                cos, sin = yturn_ref[0, k : k + 1], yturn_ref[1, k : k + 1]
                zbuf[0, pl.ds(u * 16 + k, 8, stride=16), :] = re * cos - im * sin
                zbuf[1, pl.ds(u * 16 + k, 8, stride=16), :] = re * sin + im * cos
        hi, lo = halves(jnp.concatenate([zbuf[0], zbuf[1]], axis=1))
        waves = dot_nt(yhi_ref[...], hi) + dot_nt(yhi_ref[...], lo) + dot_nt(ylo_ref[...], hi)
        ybuf[c] = waves.reshape(2, 128, 256)
        swap = remote(ybuf.at[c, 1 - core], ysib.at[c], y_send.at[c], y_recv.at[c], twin)
        swap.start()
        for half in range(2):
            if half:
                swap.wait_recv()
            for part in range(2):
                for q in range(0, 64, 8):
                    for cc in range(2):
                        spot = pl.ds(part * 64 + q, 8), pl.ds(cc * 128, 128)
                        value = ysib[(c, *spot)] if half else ybuf[(c, core, *spot)]
                        msg2[c, pl.ds(q * 8 + half * 4 + part * 2 + cc, 8, stride=8), :] = value
        local(msg2.at[c, pl.ds(chip * 8, 8)], arr2.at[c, pl.ds(chip * 8, 8)], own2_sem.at[c]).start()
        for k in range(63):
            remote(
                msg2.at[c, pl.ds(blocks[k] * 8, 8)], arr2.at[c, pl.ds(chip * 8, 8)],
                e2_send.at[c], e2_recv.at[c], targets[k],
            ).start()

    load_green.wait()
    for c in range(3):
        remote(
            msg2.at[c, pl.ds(8, 504)], arr2.at[c, pl.ds(8, 504)], e2_send.at[c], e2_recv.at[c], twin
        ).wait_recv()
        local(msg2.at[c, pl.ds(chip * 8, 8)], arr2.at[c, pl.ds(chip * 8, 8)], own2_sem.at[c]).wait()
        sources = []
        for part in range(2):
            for half in range(2):
                sources.append(
                    jnp.concatenate(
                        [arr2[c, pl.ds(half * 4 + part * 2 + cc, 64, stride=8), :] for cc in range(2)], axis=1
                    )
                )
        hi, lo = halves(jnp.concatenate(sources, axis=0).T)
        waves = dot(hi, xhi_ref[...]) + dot(lo, xhi_ref[...]) + dot(hi, xlo_ref[...])
        for k0 in range(0, 16, 8):
            v = []
            for u in range(16):
                re, im = waves[u * 16 + k0 : u * 16 + k0 + 8, :128], waves[u * 16 + k0 : u * 16 + k0 + 8, 128:]
                cos, sin = xturn_ref[0, u : u + 1], xturn_ref[1, u : u + 1]
                v.append((re * cos - im * sin, re * sin + im * cos))
            for m, (re, im) in enumerate(dft16(v)):
                spot = slice(k0, k0 + 8), slice(m * 128, m * 128 + 128)
                for a in range(3):
                    g, h = (green[(part, PAIRS[a][c], 0, *spot)] for part in range(2))
                    add_re, add_im = g * re - h * im, g * im + h * re
                    if c:
                        add_re = result[(0, a, 0, *spot)] + add_re
                        add_im = result[(1, a, 0, *spot)] + add_im
                    result[(0, a, 0, *spot)] = add_re
                    result[(1, a, 0, *spot)] = add_im

    for copy in to_twin:
        copy.wait_send()
    remote(slots_msg.at[pl.ds(1, 63)], slots_arr.at[pl.ds(1, 63)], s_send, s_recv, twin).wait_send()
    for c in range(3):
        remote(
            msg.at[c, pl.ds(1, 63)], arr.at[c, pl.ds(1, 63)], e1_send.at[c], e1_recv.at[c], twin
        ).wait_send()
        remote(ybuf.at[c, 1 - core], ysib.at[c], y_send.at[c], y_recv.at[c], twin).wait_send()
        remote(
            msg2.at[c, pl.ds(8, 504)], arr2.at[c, pl.ds(8, 504)], e2_send.at[c], e2_recv.at[c], twin
        ).wait_send()


def per_device(tiles, tile_owner, tile_slot, tile_count, green):
    dma, vmem = pltpu.SemaphoreType.DMA, pltpu.VMEM
    hbm = pl.BlockSpec(memory_space=pltpu.HBM)
    scratch = [
        vmem((1, 512), I32), vmem((1, 512), I32),
        vmem((256, 256), BF16), vmem((256, 256), BF16), vmem((256, 256), BF16), vmem((256, 256), BF16),
        vmem((2, 16, 128), F32), vmem((2, 16, 128), F32),
        vmem((2, 3, 512, 128), F32),
        vmem((2, 6, 1, 16, 2048), F32),
        vmem((3, 64, 2, 8, 128), F32),
        vmem((3, 64, 2, 2, 8, 128), F32),
        vmem((3, 64, 2, 2, 8, 128), F32),
        vmem((64, 128), F32),
        vmem((64, 128), F32),
        vmem((64, 1, 128), F32),
        vmem((64, 1, 128), F32),
        vmem((256, 1024), BF16),
        vmem((2, 256, 128), F32),
        vmem((3, 2, 128, 256), F32),
        vmem((3, 128, 256), F32),
        vmem((3, 512, 128), F32),
        vmem((3, 512, 128), F32),
        pltpu.SemaphoreType.REGULAR((2,)), dma((8,)), dma((3,)), dma(()), dma((4,)), dma((4,)), dma((4,)),
        dma((3,)), dma((3,)), dma(()), dma(()), dma((3,)), dma((3,)), dma((3,)), dma((3,)), dma((3,)),
    ]
    call = pl.pallas_call(
        kernel,
        out_shape=vmem((2, 3, 1, 16, 2048), F32),
        in_specs=[hbm] * 2 + [pl.BlockSpec(memory_space=pltpu.SMEM)] + [hbm] * 8,
        out_specs=pl.BlockSpec(memory_space=pltpu.VMEM),
        scratch_shapes=scratch,
        compiler_params=pltpu.CompilerParams(
            collective_id=0, has_side_effects=True, vmem_limit_bytes=48 << 20
        ),
    )
    def in_hbm(*arrays):
        return [pltpu.with_memory_space_constraint(jnp.asarray(a), pltpu.HBM) for a in arrays]

    line = in_hbm(tile_owner.reshape(1, 512), tile_slot.reshape(1, 512))
    return call(*line, tile_count, *in_hbm(*tables(), tiles, green))


def solution(mesh):
    line = ("gx", "gy")
    in_specs = (P(None, None, line, None), P(line, None), P(line), P(line), P(None, None, None, line, None))
    return jax.shard_map(
        per_device, mesh=mesh, in_specs=in_specs, out_specs=P(None, None, None, line, None), check_vma=False
    )
```

```python
import functools
import math

import jax
import jax.numpy as jnp
import numpy as np
from jax import lax
from jax.experimental import pallas as pl
from jax.experimental.pallas import tpu as pltpu
from jax.sharding import PartitionSpec as P

MESH = pl.DeviceIdType.MESH
F32, BF16, I32 = jnp.float32, jnp.bfloat16, jnp.int32
PAIRS = ((0, 3, 4), (3, 1, 5), (4, 5, 2))
HOPS = [((k * 45 % 64) // 16, (k * 45 % 64) // 4 % 4, k * 45 % 4) for k in range(1, 64)]
HOPS.sort(key=lambda hop: -sum(min(d, 4 - d) for d in hop))

EARLY = 2


def halves(a):
    hi = a.astype(BF16)
    return hi, (a - hi.astype(F32)).astype(BF16)


def dot(a, b):
    return lax.dot_general(a, b, (((1,), (0,)), ((), ())), preferred_element_type=F32)


def dot_nt(a, b):
    return lax.dot_general(a, b, (((1,), (1,)), ((), ())), preferred_element_type=F32)


def times(re, im, angle):
    angle %= 16
    if angle == 0:
        return re, im
    if angle == 4:
        return im, -re
    if angle == 8:
        return -re, -im
    c, s = math.cos(2 * math.pi * angle / 16), math.sin(2 * math.pi * angle / 16)
    return re * c + im * s, im * c - re * s


def dft4(v):
    (ar, ai), (br, bi), (cr, ci), (dr, di) = v
    pr, pi, qr, qi = ar + cr, ai + ci, ar - cr, ai - ci
    rr, ri, sr, si = br + dr, bi + di, br - dr, bi - di
    return [(pr + rr, pi + ri), (qr + si, qi - sr), (pr - rr, pi - ri), (qr - si, qi + sr)]


def dft16(v):
    inner = [dft4([v[4 * a + b] for a in range(4)]) for b in range(4)]
    out = [None] * 16
    for k in range(4):
        for m, value in enumerate(dft4([times(*inner[b][k], b * k) for b in range(4)])):
            out[k + 4 * m] = value
    return out


def tables():
    n = np.arange(128)
    angle = 2 * np.pi * (n[:, None] * n[None, :] % 128) / 128
    cos, sin = np.cos(angle), np.sin(angle)
    full = np.block([[cos, sin], [-sin, cos]])
    chip = np.arange(64)
    device = [(chip // 16 * 2 + core) * 16 + chip % 16 for core in range(2)]
    y_rows = np.concatenate([np.concatenate([device[core], 128 + device[core]]) for core in range(2)])
    y_table = full[y_rows]
    x_cols = [np.concatenate([part * 128 + device[s] for part in range(2) for s in (core, 1 - core)]) for core in range(2)]
    x_table = np.stack([full[:, cols].T for cols in x_cols])
    k = np.arange(16)
    turn = 2 * np.pi * k[:, None] * n[None, :] / 2048
    y_turn = np.stack([np.cos(turn), -np.sin(turn)]) / 2048
    x_turn = np.stack([np.cos(turn), -np.sin(turn)])

    def two(a):
        hi = a.astype(np.float32).astype(jnp.bfloat16)
        return hi, (a - hi.astype(np.float64)).astype(np.float32).astype(jnp.bfloat16)

    return (*two(y_table), *two(x_table), y_turn.astype(np.float32), x_turn.astype(np.float32))


def kernel(
    owner_hbm, slot_hbm, count_ref, yhi_hbm, ylo_hbm, xhi_hbm, xlo_hbm, yturn_hbm, xturn_hbm,
    tiles_ref, green_ref, result,
    owner_ref, slot_ref, yhi_ref, ylo_ref, xhi_ref, xlo_ref, yturn_ref, xturn_ref,
    tiles, green, sib, msg, arr, slots_sib, slots_in, slots_msg, slots_arr,
    one_hot, zbuf, ybuf, ysib, msg2, arr2,
    round_sem, small_sem, tile_sem, green_sem, sib_send, sib_recv, own_sem,
    e1_send, e1_recv, s_send, s_recv, y_send, y_recv, e2_send, e2_recv, own2_sem,
):
    gx, gy = lax.axis_index("gx"), lax.axis_index("gy")
    x, y, z, core = gy // 4, gx // 2, gy % 4, gx % 2
    chip = y * 16 + gy
    xs, ys, zs = ([(v + d) % 4 for d in range(4)] for v in (x, y, z))
    targets = [((ys[b] * 2 + core), (xs[a] * 4 + zs[c])) for a, b, c in HOPS]
    blocks = [ys[b] * 16 + xs[a] * 4 + zs[c] for a, b, c in HOPS]
    twin = (y * 2 + 1 - core, gy)

    def local(src, dst, sem):
        return pltpu.make_async_copy(src, dst, sem)

    def remote(src, dst, send, recv, device):
        return pltpu.make_async_remote_copy(
            src_ref=src, dst_ref=dst, send_sem=send, recv_sem=recv, device_id=device, device_id_type=MESH
        )

    x_line = [(y * 2 + core, xs[d] * 4 + z) for d in (1, 2, 3)]
    y_line = [(ys[d] * 2 + core, gy) for d in (1, 2, 3)]
    z_line = [(gx, x * 4 + zs[d]) for d in (1, 2, 3)]

    def greet(sem, devices):
        for device in devices:
            pl.semaphore_signal(sem, inc=1, device_id=device, device_id_type=MESH)

    barrier = pltpu.get_barrier_semaphore()
    greet(barrier, (twin, *x_line, *y_line, *z_line))


    small = [
        (owner_hbm, owner_ref), (slot_hbm, slot_ref),
        (yhi_hbm, yhi_ref), (ylo_hbm, ylo_ref), (xhi_hbm.at[core], xhi_ref), (xlo_hbm.at[core], xlo_ref),
        (yturn_hbm, yturn_ref), (xturn_hbm, xturn_ref),
    ]
    small = [local(src, dst, small_sem.at[k]) for k, (src, dst) in enumerate(small)]
    load_tiles = [local(tiles_ref.at[:, c], tiles.at[:, c], tile_sem.at[c]) for c in range(3)]
    load_green = local(green_ref, green, green_sem)
    for copy in (*small[:2], *load_tiles):
        copy.start()

    for copy in small[:2]:
        copy.wait()
    owner = owner_ref[...]
    side = ((owner >> 4) + core) & 1
    goal = side * 64 + ((owner >> 5) << 4) + (owner & 15)
    lane = lax.broadcasted_iota(I32, (1, 512), 1)
    goal = jnp.where(lane < count_ref[0], goal, -1)
    named = jnp.where(lax.broadcasted_iota(I32, (128, 512), 0) == goal, 1.0, 0.0)
    before = jnp.where(
        lax.broadcasted_iota(I32, (512, 512), 0) < lax.broadcasted_iota(I32, (512, 512), 1), 1.0, 0.0
    )
    counts = dot(named.astype(BF16), before.astype(BF16))
    rank = jnp.sum(named * counts, axis=0, keepdims=True).astype(I32)
    row = jnp.where(goal < 0, -1, goal * 8 + rank)
    slot = slot_ref[...]
    place = ((slot & 15) << 4) + (slot >> 4) + 1
    by_rank = jnp.where((lax.broadcasted_iota(I32, (128, 512), 0) & 7) == rank, place.astype(F32), 0.0)
    slots_out = dot_nt(named.astype(BF16), by_rank.astype(BF16))
    slots_sib[...] = slots_out[64:]
    pick = jnp.where(lax.broadcasted_iota(I32, (1024, 512), 0) == row, 1.0, 0.0).astype(BF16)

    def pack(c):
        load_tiles[c].wait()
        for part in range(2):
            hi, lo = halves(tiles[part, c])
            both = dot(pick, jnp.concatenate([hi, lo], axis=1))
            packed = (both[:, :128] + both[:, 128:]).reshape(128, 8, 128)
            msg[c, :, part, 0] = packed[:64]
            sib[c, :, part] = packed[64:]

    to_twin = [remote(sib.at[c], msg.at[c, :, :, 1], sib_send.at[c], sib_recv.at[c], twin) for c in range(3)]
    to_twin.append(remote(slots_sib, slots_in, sib_send.at[3], sib_recv.at[3], twin))
    own = [local(msg.at[c, chip], arr.at[c, 0], own_sem.at[c]) for c in range(3)]
    own.append(local(slots_msg.at[chip], slots_arr.at[0], own_sem.at[3]))
    pending = {(c, k) for c in range(3) for k in range(63)}

    def send(c, far):
        for k in range(63):
            if (c, k) in pending and sum(d > 0 for d in HOPS[k]) <= far:
                pending.discard((c, k))
                remote(msg.at[c, blocks[k]], arr.at[c, k + 1], e1_send.at[c], e1_recv.at[c], targets[k]).start()
                if c == 1:
                    remote(slots_msg.at[blocks[k]], slots_arr.at[k + 1], s_send, s_recv, targets[k]).start()

    pack(0)
    pl.semaphore_wait(barrier, 10)
    greet(round_sem.at[0], (*x_line, *y_line, *z_line))
    to_twin[3].start()
    to_twin[0].start()
    pack(1)
    to_twin[1].start()
    pack(2)
    to_twin[2].start()
    for copy in (*small[2:], load_green):
        copy.start()
    pl.semaphore_wait(round_sem.at[0], 9)
    greet(round_sem.at[1], x_line)
    to_twin[0].wait_recv()
    own[0].start()
    send(0, EARLY)
    to_twin[3].wait_recv()
    lanes = lax.broadcasted_iota(I32, (64, 128), 1)
    slots_msg[:, 0, :] = jnp.where(lanes < 64, slots_out[:64], slots_in[...])
    own[3].start()
    pl.semaphore_wait(round_sem.at[1], 3)
    send(0, 3)
    for c in (1, 2):
        to_twin[c].wait_recv()
        own[c].start()
        send(c, 3)

    for copy in small[2:]:
        copy.wait()
    remote(slots_msg.at[pl.ds(1, 63)], slots_arr.at[pl.ds(1, 63)], s_send, s_recv, twin).wait_recv()
    own[3].wait()
    spread = jnp.where(
        lax.broadcasted_iota(I32, (1024, 64), 0) >> 4 == lax.broadcasted_iota(I32, (1024, 64), 1), 1.0, 0.0
    ).astype(BF16)
    arrived = dot(spread, slots_arr[:, 0, :].astype(BF16))
    tile_id = lax.broadcasted_iota(I32, (1024, 128), 0)
    mine = lax.broadcasted_iota(I32, (1024, 128), 1) == ((tile_id >> 3) & 1) * 64 + (tile_id & 7)
    arrived = jnp.where(mine, arrived, 0.0).astype(BF16)
    place_of = dot_nt(jnp.ones((256, 128), BF16), arrived)
    one_hot[...] = jnp.where(
        place_of == (lax.broadcasted_iota(I32, (256, 1024), 0) + 1).astype(F32), 1.0, 0.0
    ).astype(BF16)

    for c in range(3):
        remote(
            msg.at[c, pl.ds(1, 63)], arr.at[c, pl.ds(1, 63)], e1_send.at[c], e1_recv.at[c], twin
        ).wait_recv()
        own[c].wait()
        slab = []
        for part in range(2):
            hi, lo = halves(arr[c, :, part].reshape(1024, 128))
            both = dot(one_hot[...], jnp.concatenate([hi, lo], axis=1))
            slab.append(both[:, :128] + both[:, 128:])
        for u in range(0, 16, 8):
            v = [(slab[0][16 * t + u : 16 * t + u + 8], slab[1][16 * t + u : 16 * t + u + 8]) for t in range(16)]
            for k, (re, im) in enumerate(dft16(v)):
                cos, sin = yturn_ref[0, k : k + 1], yturn_ref[1, k : k + 1]
                zbuf[0, pl.ds(u * 16 + k, 8, stride=16), :] = re * cos - im * sin
                zbuf[1, pl.ds(u * 16 + k, 8, stride=16), :] = re * sin + im * cos
        hi, lo = halves(jnp.concatenate([zbuf[0], zbuf[1]], axis=1))
        waves = dot_nt(yhi_ref[...], hi) + dot_nt(yhi_ref[...], lo) + dot_nt(ylo_ref[...], hi)
        ybuf[c] = waves.reshape(2, 128, 256)
        swap = remote(ybuf.at[c, 1 - core], ysib.at[c], y_send.at[c], y_recv.at[c], twin)
        swap.start()
        for half in range(2):
            if half:
                swap.wait_recv()
            for part in range(2):
                for q in range(0, 64, 8):
                    for cc in range(2):
                        spot = pl.ds(part * 64 + q, 8), pl.ds(cc * 128, 128)
                        value = ysib[(c, *spot)] if half else ybuf[(c, core, *spot)]
                        msg2[c, pl.ds(q * 8 + half * 4 + part * 2 + cc, 8, stride=8), :] = value
        local(msg2.at[c, pl.ds(chip * 8, 8)], arr2.at[c, pl.ds(chip * 8, 8)], own2_sem.at[c]).start()
        for k in range(63):
            remote(
                msg2.at[c, pl.ds(blocks[k] * 8, 8)], arr2.at[c, pl.ds(chip * 8, 8)],
                e2_send.at[c], e2_recv.at[c], targets[k],
            ).start()

    load_green.wait()
    for c in range(3):
        remote(
            msg2.at[c, pl.ds(8, 504)], arr2.at[c, pl.ds(8, 504)], e2_send.at[c], e2_recv.at[c], twin
        ).wait_recv()
        local(msg2.at[c, pl.ds(chip * 8, 8)], arr2.at[c, pl.ds(chip * 8, 8)], own2_sem.at[c]).wait()
        sources = []
        for part in range(2):
            for half in range(2):
                sources.append(
                    jnp.concatenate(
                        [arr2[c, pl.ds(half * 4 + part * 2 + cc, 64, stride=8), :] for cc in range(2)], axis=1
                    )
                )
        hi, lo = halves(jnp.concatenate(sources, axis=0).T)
        waves = dot(hi, xhi_ref[...]) + dot(lo, xhi_ref[...]) + dot(hi, xlo_ref[...])
        for k0 in range(0, 16, 8):
            v = []
            for u in range(16):
                re, im = waves[u * 16 + k0 : u * 16 + k0 + 8, :128], waves[u * 16 + k0 : u * 16 + k0 + 8, 128:]
                cos, sin = xturn_ref[0, u : u + 1], xturn_ref[1, u : u + 1]
                v.append((re * cos - im * sin, re * sin + im * cos))
            for m, (re, im) in enumerate(dft16(v)):
                spot = slice(k0, k0 + 8), slice(m * 128, m * 128 + 128)
                for a in range(3):
                    g, h = (green[(part, PAIRS[a][c], 0, *spot)] for part in range(2))
                    add_re, add_im = g * re - h * im, g * im + h * re
                    if c:
                        add_re = result[(0, a, 0, *spot)] + add_re
                        add_im = result[(1, a, 0, *spot)] + add_im
                    result[(0, a, 0, *spot)] = add_re
                    result[(1, a, 0, *spot)] = add_im

    for copy in to_twin:
        copy.wait_send()
    remote(slots_msg.at[pl.ds(1, 63)], slots_arr.at[pl.ds(1, 63)], s_send, s_recv, twin).wait_send()
    for c in range(3):
        remote(
            msg.at[c, pl.ds(1, 63)], arr.at[c, pl.ds(1, 63)], e1_send.at[c], e1_recv.at[c], twin
        ).wait_send()
        remote(ybuf.at[c, 1 - core], ysib.at[c], y_send.at[c], y_recv.at[c], twin).wait_send()
        remote(
            msg2.at[c, pl.ds(8, 504)], arr2.at[c, pl.ds(8, 504)], e2_send.at[c], e2_recv.at[c], twin
        ).wait_send()


def per_device(tiles, tile_owner, tile_slot, tile_count, green):
    dma, vmem = pltpu.SemaphoreType.DMA, pltpu.VMEM
    hbm = pl.BlockSpec(memory_space=pltpu.HBM)
    scratch = [
        vmem((1, 512), I32), vmem((1, 512), I32),
        vmem((256, 256), BF16), vmem((256, 256), BF16), vmem((256, 256), BF16), vmem((256, 256), BF16),
        vmem((2, 16, 128), F32), vmem((2, 16, 128), F32),
        vmem((2, 3, 512, 128), F32),
        vmem((2, 6, 1, 16, 2048), F32),
        vmem((3, 64, 2, 8, 128), F32),
        vmem((3, 64, 2, 2, 8, 128), F32),
        vmem((3, 64, 2, 2, 8, 128), F32),
        vmem((64, 128), F32),
        vmem((64, 128), F32),
        vmem((64, 1, 128), F32),
        vmem((64, 1, 128), F32),
        vmem((256, 1024), BF16),
        vmem((2, 256, 128), F32),
        vmem((3, 2, 128, 256), F32),
        vmem((3, 128, 256), F32),
        vmem((3, 512, 128), F32),
        vmem((3, 512, 128), F32),
        pltpu.SemaphoreType.REGULAR((2,)), dma((8,)), dma((3,)), dma(()), dma((4,)), dma((4,)), dma((4,)),
        dma((3,)), dma((3,)), dma(()), dma(()), dma((3,)), dma((3,)), dma((3,)), dma((3,)), dma((3,)),
    ]
    call = pl.pallas_call(
        kernel,
        out_shape=vmem((2, 3, 1, 16, 2048), F32),
        in_specs=[hbm] * 2 + [pl.BlockSpec(memory_space=pltpu.SMEM)] + [hbm] * 8,
        out_specs=pl.BlockSpec(memory_space=pltpu.VMEM),
        scratch_shapes=scratch,
        compiler_params=pltpu.CompilerParams(
            collective_id=0, has_side_effects=True, vmem_limit_bytes=48 << 20
        ),
    )
    def in_hbm(*arrays):
        return [pltpu.with_memory_space_constraint(jnp.asarray(a), pltpu.HBM) for a in arrays]

    line = in_hbm(tile_owner.reshape(1, 512), tile_slot.reshape(1, 512))
    return call(*line, tile_count, *in_hbm(*tables(), tiles, green))


def solution(mesh):
    line = ("gx", "gy")
    in_specs = (P(None, None, line, None), P(line, None), P(line), P(line), P(None, None, None, line, None))
    return jax.shard_map(
        per_device, mesh=mesh, in_specs=in_specs, out_specs=P(None, None, None, line, None), check_vma=False
    )
```

```python
import functools
import math

import jax
import jax.numpy as jnp
import numpy as np
from jax import lax
from jax.experimental import pallas as pl
from jax.experimental.pallas import tpu as pltpu
from jax.sharding import PartitionSpec as P

MESH = pl.DeviceIdType.MESH
F32, BF16, I32 = jnp.float32, jnp.bfloat16, jnp.int32
PAIRS = ((0, 3, 4), (3, 1, 5), (4, 5, 2))
HOPS = [((k * 45 % 64) // 16, (k * 45 % 64) // 4 % 4, k * 45 % 4) for k in range(1, 64)]
HOPS.sort(key=lambda hop: -sum(min(d, 4 - d) for d in hop))

EARLY = 2


def halves(a):
    hi = a.astype(BF16)
    return hi, (a - hi.astype(F32)).astype(BF16)


def dot(a, b):
    return lax.dot_general(a, b, (((1,), (0,)), ((), ())), preferred_element_type=F32)


def dot_nt(a, b):
    return lax.dot_general(a, b, (((1,), (1,)), ((), ())), preferred_element_type=F32)


def times(re, im, angle):
    angle %= 16
    if angle == 0:
        return re, im
    if angle == 4:
        return im, -re
    if angle == 8:
        return -re, -im
    c, s = math.cos(2 * math.pi * angle / 16), math.sin(2 * math.pi * angle / 16)
    return re * c + im * s, im * c - re * s


def dft4(v):
    (ar, ai), (br, bi), (cr, ci), (dr, di) = v
    pr, pi, qr, qi = ar + cr, ai + ci, ar - cr, ai - ci
    rr, ri, sr, si = br + dr, bi + di, br - dr, bi - di
    return [(pr + rr, pi + ri), (qr + si, qi - sr), (pr - rr, pi - ri), (qr - si, qi + sr)]


def dft16(v):
    inner = [dft4([v[4 * a + b] for a in range(4)]) for b in range(4)]
    out = [None] * 16
    for k in range(4):
        for m, value in enumerate(dft4([times(*inner[b][k], b * k) for b in range(4)])):
            out[k + 4 * m] = value
    return out


def tables():
    n = np.arange(128)
    angle = 2 * np.pi * (n[:, None] * n[None, :] % 128) / 128
    cos, sin = np.cos(angle), np.sin(angle)
    full = np.block([[cos, sin], [-sin, cos]])
    chip = np.arange(64)
    device = [(chip // 16 * 2 + core) * 16 + chip % 16 for core in range(2)]
    y_rows = np.concatenate([np.concatenate([device[core], 128 + device[core]]) for core in range(2)])
    y_table = full[y_rows]
    x_cols = [np.concatenate([part * 128 + device[s] for part in range(2) for s in (core, 1 - core)]) for core in range(2)]
    x_table = np.stack([full[:, cols].T for cols in x_cols])
    k = np.arange(16)
    turn = 2 * np.pi * k[:, None] * n[None, :] / 2048
    y_turn = np.stack([np.cos(turn), -np.sin(turn)]) / 2048
    x_turn = np.stack([np.cos(turn), -np.sin(turn)])

    def two(a):
        hi = a.astype(np.float32).astype(jnp.bfloat16)
        return hi, (a - hi.astype(np.float64)).astype(np.float32).astype(jnp.bfloat16)

    return (*two(y_table), *two(x_table), y_turn.astype(np.float32), x_turn.astype(np.float32))


def kernel(
    owner_hbm, slot_hbm, count_ref, yhi_hbm, ylo_hbm, xhi_hbm, xlo_hbm, yturn_hbm, xturn_hbm,
    tiles_ref, green_ref, result,
    owner_ref, slot_ref, yhi_ref, ylo_ref, xhi_ref, xlo_ref, yturn_ref, xturn_ref,
    tiles, green, sib, msg, arr, slots_sib, slots_in, slots_msg, slots_arr,
    one_hot, zbuf, ybuf, ysib, msg2, arr2,
    round_sem, small_sem, tile_sem, green_sem, sib_send, sib_recv, own_sem,
    e1_send, e1_recv, s_send, s_recv, y_send, y_recv, e2_send, e2_recv, own2_sem,
):
    gx, gy = lax.axis_index("gx"), lax.axis_index("gy")
    x, y, z, core = gy // 4, gx // 2, gy % 4, gx % 2
    chip = y * 16 + gy
    xs, ys, zs = ([(v + d) % 4 for d in range(4)] for v in (x, y, z))
    targets = [((ys[b] * 2 + core), (xs[a] * 4 + zs[c])) for a, b, c in HOPS]
    blocks = [ys[b] * 16 + xs[a] * 4 + zs[c] for a, b, c in HOPS]
    twin = (y * 2 + 1 - core, gy)

    def local(src, dst, sem):
        return pltpu.make_async_copy(src, dst, sem)

    def remote(src, dst, send, recv, device):
        return pltpu.make_async_remote_copy(
            src_ref=src, dst_ref=dst, send_sem=send, recv_sem=recv, device_id=device, device_id_type=MESH
        )

    small = [
        (owner_hbm, owner_ref), (slot_hbm, slot_ref),
        (yhi_hbm, yhi_ref), (ylo_hbm, ylo_ref), (xhi_hbm.at[core], xhi_ref), (xlo_hbm.at[core], xlo_ref),
        (yturn_hbm, yturn_ref), (xturn_hbm, xturn_ref),
    ]
    small = [local(src, dst, small_sem.at[k]) for k, (src, dst) in enumerate(small)]
    load_tiles = [local(tiles_ref.at[:, c], tiles.at[:, c], tile_sem.at[c]) for c in range(3)]
    load_green = local(green_ref, green, green_sem)
    for copy in (*small[:2], *load_tiles, *small[2:], load_green):
        copy.start()

    x_line = [(y * 2 + core, xs[d] * 4 + z) for d in (1, 2, 3)]
    y_line = [(ys[d] * 2 + core, gy) for d in (1, 2, 3)]
    z_line = [(gx, x * 4 + zs[d]) for d in (1, 2, 3)]

    def greet(sem, devices):
        for device in devices:
            pl.semaphore_signal(sem, inc=1, device_id=device, device_id_type=MESH)

    barrier = pltpu.get_barrier_semaphore()
    greet(barrier, (twin, *x_line, *y_line, *z_line))

    for copy in small[:2]:
        copy.wait()
    owner = owner_ref[...]
    side = ((owner >> 4) + core) & 1
    goal = side * 64 + ((owner >> 5) << 4) + (owner & 15)
    lane = lax.broadcasted_iota(I32, (1, 512), 1)
    goal = jnp.where(lane < count_ref[0], goal, -1)
    named = jnp.where(lax.broadcasted_iota(I32, (128, 512), 0) == goal, 1.0, 0.0)
    before = jnp.where(
        lax.broadcasted_iota(I32, (512, 512), 0) < lax.broadcasted_iota(I32, (512, 512), 1), 1.0, 0.0
    )
    counts = dot(named.astype(BF16), before.astype(BF16))
    rank = jnp.sum(named * counts, axis=0, keepdims=True).astype(I32)
    row = jnp.where(goal < 0, -1, goal * 8 + rank)
    slot = slot_ref[...]
    place = ((slot & 15) << 4) + (slot >> 4) + 1
    by_rank = jnp.where((lax.broadcasted_iota(I32, (128, 512), 0) & 7) == rank, place.astype(F32), 0.0)
    slots_out = dot_nt(named.astype(BF16), by_rank.astype(BF16))
    slots_sib[...] = slots_out[64:]
    pick = jnp.where(lax.broadcasted_iota(I32, (1024, 512), 0) == row, 1.0, 0.0).astype(BF16)

    def pack(c):
        load_tiles[c].wait()
        for part in range(2):
            hi, lo = halves(tiles[part, c])
            both = dot(pick, jnp.concatenate([hi, lo], axis=1))
            packed = (both[:, :128] + both[:, 128:]).reshape(128, 8, 128)
            msg[c, :, part, 0] = packed[:64]
            sib[c, :, part] = packed[64:]

    to_twin = [remote(sib.at[c], msg.at[c, :, :, 1], sib_send.at[c], sib_recv.at[c], twin) for c in range(3)]
    to_twin.append(remote(slots_sib, slots_in, sib_send.at[3], sib_recv.at[3], twin))
    own = [local(msg.at[c, chip], arr.at[c, 0], own_sem.at[c]) for c in range(3)]
    own.append(local(slots_msg.at[chip], slots_arr.at[0], own_sem.at[3]))
    pending = {(c, k) for c in range(3) for k in range(63)}

    def send(c, far):
        for k in range(63):
            if (c, k) in pending and sum(d > 0 for d in HOPS[k]) <= far:
                pending.discard((c, k))
                remote(msg.at[c, blocks[k]], arr.at[c, k + 1], e1_send.at[c], e1_recv.at[c], targets[k]).start()
                if c == 1:
                    remote(slots_msg.at[blocks[k]], slots_arr.at[k + 1], s_send, s_recv, targets[k]).start()

    pack(0)
    pl.semaphore_wait(barrier, 10)
    greet(round_sem.at[0], (*x_line, *y_line, *z_line))
    to_twin[3].start()
    to_twin[0].start()
    pack(1)
    to_twin[1].start()
    pack(2)
    to_twin[2].start()
    pl.semaphore_wait(round_sem.at[0], 9)
    greet(round_sem.at[1], x_line)
    to_twin[0].wait_recv()
    own[0].start()
    send(0, EARLY)
    to_twin[3].wait_recv()
    lanes = lax.broadcasted_iota(I32, (64, 128), 1)
    slots_msg[:, 0, :] = jnp.where(lanes < 64, slots_out[:64], slots_in[...])
    own[3].start()
    pl.semaphore_wait(round_sem.at[1], 3)
    send(0, 3)
    for c in (1, 2):
        to_twin[c].wait_recv()
        own[c].start()
        send(c, 3)

    for copy in small[2:]:
        copy.wait()
    remote(slots_msg.at[pl.ds(1, 63)], slots_arr.at[pl.ds(1, 63)], s_send, s_recv, twin).wait_recv()
    own[3].wait()
    spread = jnp.where(
        lax.broadcasted_iota(I32, (1024, 64), 0) >> 4 == lax.broadcasted_iota(I32, (1024, 64), 1), 1.0, 0.0
    ).astype(BF16)
    arrived = dot(spread, slots_arr[:, 0, :].astype(BF16))
    tile_id = lax.broadcasted_iota(I32, (1024, 128), 0)
    mine = lax.broadcasted_iota(I32, (1024, 128), 1) == ((tile_id >> 3) & 1) * 64 + (tile_id & 7)
    arrived = jnp.where(mine, arrived, 0.0).astype(BF16)
    place_of = dot_nt(jnp.ones((256, 128), BF16), arrived)
    one_hot[...] = jnp.where(
        place_of == (lax.broadcasted_iota(I32, (256, 1024), 0) + 1).astype(F32), 1.0, 0.0
    ).astype(BF16)

    def scatter(c):
        local(msg2.at[c, pl.ds(chip * 8, 8)], arr2.at[c, pl.ds(chip * 8, 8)], own2_sem.at[c]).start()
        for k in range(63):
            remote(
                msg2.at[c, pl.ds(blocks[k] * 8, 8)], arr2.at[c, pl.ds(chip * 8, 8)],
                e2_send.at[c], e2_recv.at[c], targets[k],
            ).start()

    for c in range(3):
        remote(
            msg.at[c, pl.ds(1, 63)], arr.at[c, pl.ds(1, 63)], e1_send.at[c], e1_recv.at[c], twin
        ).wait_recv()
        own[c].wait()
        if c:
            scatter(c - 1)
        slab = []
        for part in range(2):
            hi, lo = halves(arr[c, :, part].reshape(1024, 128))
            both = dot(one_hot[...], jnp.concatenate([hi, lo], axis=1))
            slab.append(both[:, :128] + both[:, 128:])
        for u in range(0, 16, 8):
            v = [(slab[0][16 * t + u : 16 * t + u + 8], slab[1][16 * t + u : 16 * t + u + 8]) for t in range(16)]
            for k, (re, im) in enumerate(dft16(v)):
                cos, sin = yturn_ref[0, k : k + 1], yturn_ref[1, k : k + 1]
                zbuf[0, pl.ds(u * 16 + k, 8, stride=16), :] = re * cos - im * sin
                zbuf[1, pl.ds(u * 16 + k, 8, stride=16), :] = re * sin + im * cos
        hi, lo = halves(jnp.concatenate([zbuf[0], zbuf[1]], axis=1))
        waves = dot_nt(yhi_ref[...], hi) + dot_nt(yhi_ref[...], lo) + dot_nt(ylo_ref[...], hi)
        ybuf[c] = waves.reshape(2, 128, 256)
        swap = remote(ybuf.at[c, 1 - core], ysib.at[c], y_send.at[c], y_recv.at[c], twin)
        swap.start()
        for half in range(2):
            if half:
                swap.wait_recv()
            for part in range(2):
                for q in range(0, 64, 8):
                    for cc in range(2):
                        spot = pl.ds(part * 64 + q, 8), pl.ds(cc * 128, 128)
                        value = ysib[(c, *spot)] if half else ybuf[(c, core, *spot)]
                        msg2[c, pl.ds(q * 8 + half * 4 + part * 2 + cc, 8, stride=8), :] = value
        if c == 2:
            scatter(2)

    load_green.wait()
    for c in range(3):
        remote(
            msg2.at[c, pl.ds(8, 504)], arr2.at[c, pl.ds(8, 504)], e2_send.at[c], e2_recv.at[c], twin
        ).wait_recv()
        local(msg2.at[c, pl.ds(chip * 8, 8)], arr2.at[c, pl.ds(chip * 8, 8)], own2_sem.at[c]).wait()
        sources = []
        for part in range(2):
            for half in range(2):
                sources.append(
                    jnp.concatenate(
                        [arr2[c, pl.ds(half * 4 + part * 2 + cc, 64, stride=8), :] for cc in range(2)], axis=1
                    )
                )
        hi, lo = halves(jnp.concatenate(sources, axis=0).T)
        waves = dot(hi, xhi_ref[...]) + dot(lo, xhi_ref[...]) + dot(hi, xlo_ref[...])
        for k0 in range(0, 16, 8):
            v = []
            for u in range(16):
                re, im = waves[u * 16 + k0 : u * 16 + k0 + 8, :128], waves[u * 16 + k0 : u * 16 + k0 + 8, 128:]
                cos, sin = xturn_ref[0, u : u + 1], xturn_ref[1, u : u + 1]
                v.append((re * cos - im * sin, re * sin + im * cos))
            for m, (re, im) in enumerate(dft16(v)):
                spot = slice(k0, k0 + 8), slice(m * 128, m * 128 + 128)
                for a in range(3):
                    g, h = (green[(part, PAIRS[a][c], 0, *spot)] for part in range(2))
                    add_re, add_im = g * re - h * im, g * im + h * re
                    if c:
                        add_re = result[(0, a, 0, *spot)] + add_re
                        add_im = result[(1, a, 0, *spot)] + add_im
                    result[(0, a, 0, *spot)] = add_re
                    result[(1, a, 0, *spot)] = add_im

    for copy in to_twin:
        copy.wait_send()
    remote(slots_msg.at[pl.ds(1, 63)], slots_arr.at[pl.ds(1, 63)], s_send, s_recv, twin).wait_send()
    for c in range(3):
        remote(
            msg.at[c, pl.ds(1, 63)], arr.at[c, pl.ds(1, 63)], e1_send.at[c], e1_recv.at[c], twin
        ).wait_send()
        remote(ybuf.at[c, 1 - core], ysib.at[c], y_send.at[c], y_recv.at[c], twin).wait_send()
        remote(
            msg2.at[c, pl.ds(8, 504)], arr2.at[c, pl.ds(8, 504)], e2_send.at[c], e2_recv.at[c], twin
        ).wait_send()


def per_device(tiles, tile_owner, tile_slot, tile_count, green):
    dma, vmem = pltpu.SemaphoreType.DMA, pltpu.VMEM
    hbm = pl.BlockSpec(memory_space=pltpu.HBM)
    scratch = [
        vmem((1, 512), I32), vmem((1, 512), I32),
        vmem((256, 256), BF16), vmem((256, 256), BF16), vmem((256, 256), BF16), vmem((256, 256), BF16),
        vmem((2, 16, 128), F32), vmem((2, 16, 128), F32),
        vmem((2, 3, 512, 128), F32),
        vmem((2, 6, 1, 16, 2048), F32),
        vmem((3, 64, 2, 8, 128), F32),
        vmem((3, 64, 2, 2, 8, 128), F32),
        vmem((3, 64, 2, 2, 8, 128), F32),
        vmem((64, 128), F32),
        vmem((64, 128), F32),
        vmem((64, 1, 128), F32),
        vmem((64, 1, 128), F32),
        vmem((256, 1024), BF16),
        vmem((2, 256, 128), F32),
        vmem((3, 2, 128, 256), F32),
        vmem((3, 128, 256), F32),
        vmem((3, 512, 128), F32),
        vmem((3, 512, 128), F32),
        pltpu.SemaphoreType.REGULAR((2,)), dma((8,)), dma((3,)), dma(()), dma((4,)), dma((4,)), dma((4,)),
        dma((3,)), dma((3,)), dma(()), dma(()), dma((3,)), dma((3,)), dma((3,)), dma((3,)), dma((3,)),
    ]
    call = pl.pallas_call(
        kernel,
        out_shape=vmem((2, 3, 1, 16, 2048), F32),
        in_specs=[hbm] * 2 + [pl.BlockSpec(memory_space=pltpu.SMEM)] + [hbm] * 8,
        out_specs=pl.BlockSpec(memory_space=pltpu.VMEM),
        scratch_shapes=scratch,
        compiler_params=pltpu.CompilerParams(
            collective_id=0, has_side_effects=True, vmem_limit_bytes=48 << 20
        ),
    )
    def in_hbm(*arrays):
        return [pltpu.with_memory_space_constraint(jnp.asarray(a), pltpu.HBM) for a in arrays]

    line = in_hbm(tile_owner.reshape(1, 512), tile_slot.reshape(1, 512))
    return call(*line, tile_count, *in_hbm(*tables(), tiles, green))


def solution(mesh):
    line = ("gx", "gy")
    in_specs = (P(None, None, line, None), P(line, None), P(line), P(line), P(None, None, None, line, None))
    return jax.shard_map(
        per_device, mesh=mesh, in_specs=in_specs, out_specs=P(None, None, None, line, None), check_vma=False
    )
```
